256 devices in a mesh: gx: 8 (over z), gy: 32 (over x, y, core).
Axes of the slice: x: 4, y: 4, z: 8, core: 2. Of those that a mesh axis runs over, the one named last changes fastest.
Arguments:
- sources: float32 [8192, 4, 256], P(('gx', 'gy')), may hold values from -1 to 1, as said below
- live_counts: int32 [8192], P(('gx', 'gy')), may hold values from 1 to 256, as said below
- densities: float32 [296, 8192], P(None, ('gx', 'gy')), may hold values from -0.75 to 0.75
- near_list: int32 [8192, 4], P(('gx', 'gy')), may hold values from 0 to 8191, as said below
- far_list: int32 [8192, 16], P(('gx', 'gy')), may hold values from 0 to 8191, as said below
- far_class: int32 [8192, 16], P(('gx', 'gy')), may hold values from 0 to 15
- coarse_list: int32 [8192, 8], P(('gx', 'gy')), may hold values from 0 to 1023
- coarse_class: int32 [8192, 8], P(('gx', 'gy')), may hold values from 0 to 15
- translations: float32 [16, 296, 296], replicated, may hold values from -0.375 to 0.375
- check_to_equiv: float32 [296, 296], replicated, may hold values from -0.375 to 0.375
- up_check_to_equiv: float32 [296, 296], replicated, may hold values from -0.375 to 0.375
- partial_check: float32 [256, 296, 64], P(('gx', 'gy')), may hold values from -0.1875 to 0.1875
- contrib_ids: int32 [256, 64], P(('gx', 'gy')), may hold values from 0 to 1023, as said below
Outputs:
- potential: float32 [8192, 256], P(('gx', 'gy'))
The draws below stay inside these ranges and needn't reach their ends.
Inputs may be any that keep to these rules, and one draw needn't show every extreme that they name: `near_list`: entry 0 of a leaf's row is the leaf itself; the others are distinct other leaves whose numbers differ from it by at most 32. `far_list`: A leaf's entries are distinct other leaves whose numbers differ from it by at most 32. `live_counts`: some leaf holds exactly 256 live points. `sources`: rows 0 to 2 lie in -1 to 1. `contrib_ids`: row d names only shared octants s with d - 1 <= floor(s * 256 / 1024) <= d + 1; a number may repeat.
All inputs are finite; a program needn't handle non-finite values.
Results may differ from the reference program's by a relative error of at most 0.0003.
Values sent between devices are 32-bit elements; how exact they have to be, the bound alone decides.
A program may use at most 64 MiB of HBM per device.

```python
import jax
import jax.numpy as jnp
import numpy as np
from jax import lax

ORDER = 8
P_SIZE = 296
LEAF = 256
OCT_DEV = 32
NEAR = 4
FAR = 16
COARSE = 8
CLASSES = 16
SHARED = 1024
CONTRIB = 64
OWNERS = 256
NLEAF = 8192


def window_picks(key, picks_count):
    leaf_total = NLEAF
    span_width = 2 * OCT_DEV + 1
    leaf_ids = jnp.arange(leaf_total, dtype=jnp.int32)
    offsets = jnp.arange(span_width, dtype=jnp.int32) - OCT_DEV
    reached = leaf_ids[:, None] + offsets[None, :]
    usable = (reached >= 0) & (reached < leaf_total) & (offsets[None, :] != 0)
    scores = jax.random.randint(key, (leaf_total, span_width), 0, 2 ** 20, dtype=jnp.int32) * 1024 + jnp.arange(span_width, dtype=jnp.int32)[None, :]
    forced = (leaf_ids[:, None] == 1) & (offsets[None, :] == -1) | (leaf_ids[:, None] == leaf_total - 2) & (offsets[None, :] == 1)
    scores = jnp.where(forced, 2 ** 30, scores)
    scores = jnp.where(usable, scores, -1)
    chosen = lax.top_k(scores, picks_count)[1].astype(jnp.int32)
    return (leaf_ids[:, None] + jnp.take(offsets, chosen)).astype(jnp.int32)


def draw_near_list(key, part):
    leaf_ids = jnp.arange(NLEAF, dtype=jnp.int32)
    others = window_picks(jax.random.fold_in(key, 31), NEAR - 1)
    return jnp.concatenate([leaf_ids[:, None], others], axis=1).astype(jnp.int32)


def draw_far_list(key, part):
    return window_picks(jax.random.fold_in(key, 41), FAR)


def draw_live_counts(key, part):
    owners = NLEAF // OCT_DEV
    caps = jax.random.randint(jax.random.fold_in(key, 11), (owners,), LEAF // 4, LEAF + 1, dtype=jnp.int32)
    raw_counts = jax.random.randint(jax.random.fold_in(key, 12), (NLEAF,), 0, 2 ** 20, dtype=jnp.int32)
    counts = raw_counts % jnp.repeat(caps, OCT_DEV) + 1
    full_leaf = jax.random.randint(jax.random.fold_in(key, 13), (), 0, NLEAF, dtype=jnp.int32)
    return jnp.where(jnp.arange(NLEAF, dtype=jnp.int32) == full_leaf, LEAF, counts).astype(jnp.int32)


def draw_sources(key, part):
    positions = jax.random.uniform(jax.random.fold_in(key, 21), (NLEAF, 3, LEAF), jnp.float32, -1.0, 1.0)
    charges = 0.1 * jnp.clip(jax.random.normal(jax.random.fold_in(key, 22), (NLEAF, LEAF), jnp.float32), -6.0, 6.0)
    return jnp.concatenate([positions, charges[:, None, :]], axis=1).astype(jnp.float32)


def draw_contrib_ids(key, part):
    owners = NLEAF // OCT_DEV
    share_width = SHARED // owners
    owner_ids = jnp.arange(owners, dtype=jnp.int32)
    offsets = jax.random.randint(jax.random.fold_in(key, 51), (owners, CONTRIB), -1, 2, dtype=jnp.int32)
    homes = jnp.clip(owner_ids[:, None] + offsets, 0, owners - 1)
    within = jax.random.randint(jax.random.fold_in(key, 52), (owners, CONTRIB), 0, share_width, dtype=jnp.int32)
    picked = homes * share_width + within
    slot_ids = jnp.arange(CONTRIB, dtype=jnp.int32)
    picked = jnp.where((owner_ids[:, None] == 0) & (slot_ids[None, :] == 0), 0, picked)
    picked = jnp.where((owner_ids[:, None] == owners - 1) & (slot_ids[None, :] == 0), SHARED - 1, picked)
    return picked.astype(jnp.int32)


def plant(array, rng, low, top_value):
    dims = array.shape
    index_at = [jax.random.randint(jax.random.fold_in(rng, axis), (), 0, dims[axis]) for axis in range(len(dims))]
    array = array.at[tuple(index_at)].set(low)
    longest = dims.index(max(dims))
    index_at[longest] = (index_at[longest] + 1) % dims[longest]
    return array.at[tuple(index_at)].set(top_value)


def level_of(key, shape, shards, least, top_value):
    gain, own = 1.0, jax.random.fold_in(key, 6)
    for dim, parts in shards:
        heights = jnp.exp(jax.random.uniform(jax.random.fold_in(own, dim), (parts,), jnp.float32, least / len(shards), top_value / len(shards)))
        gain = gain * jnp.repeat(heights, shape[dim] // parts).reshape([-1 if axis == dim else 1 for axis in range(len(shape))])
    return gain


def bell_draw(own_key, shape, deviation, bound, split=(), kind=jnp.bfloat16):
    level = level_of(own_key, shape, split, -0.22, 0.18) if split else 1.0
    result = jax.random.normal(own_key, shape, jnp.float32) * deviation * level
    return jnp.minimum(jnp.maximum(result, -bound), bound).astype(kind)


def setup_inputs(seed: int = 0) -> dict:
    keys = jax.random.split(jax.random.key(seed), 14)
    sources = draw_sources(jax.random.fold_in(keys[13], 71), 0)
    live_counts = draw_live_counts(jax.random.fold_in(keys[13], 71), 0)
    densities = bell_draw(keys[2], (P_SIZE, NLEAF), 0.05, 0.75, ((1, 256),), jnp.float32)
    near_list = draw_near_list(jax.random.fold_in(keys[13], 71), 0)
    far_list = draw_far_list(jax.random.fold_in(keys[13], 71), 0)
    far_class = plant(jax.random.randint(keys[5], (NLEAF, FAR), 0, CLASSES), jax.random.fold_in(keys[5], 1), 0, CLASSES - 1).astype(jnp.int32)
    coarse_list = plant(jax.random.randint(keys[6], (NLEAF, COARSE), 0, SHARED), jax.random.fold_in(keys[6], 1), 0, SHARED - 1).astype(jnp.int32)
    coarse_class = plant(jax.random.randint(keys[7], (NLEAF, COARSE), 0, CLASSES), jax.random.fold_in(keys[7], 1), 0, CLASSES - 1).astype(jnp.int32)
    translations = bell_draw(keys[8], (CLASSES, P_SIZE, P_SIZE), P_SIZE ** -0.5, 0.375, (), jnp.float32)
    check_to_equiv = bell_draw(keys[9], (P_SIZE, P_SIZE), P_SIZE ** -0.5, 0.375, (), jnp.float32)
    up_check_to_equiv = bell_draw(keys[10], (P_SIZE, P_SIZE), P_SIZE ** -0.5, 0.375, (), jnp.float32)
    partial_check = bell_draw(keys[11], (OWNERS, P_SIZE, CONTRIB), (0.048 * (SHARED / (CONTRIB * OWNERS)) ** 0.5), 0.1875, ((0, 256),), jnp.float32)
    contrib_ids = draw_contrib_ids(jax.random.fold_in(keys[13], 71), 0)
    return {"sources": sources, "live_counts": live_counts, "densities": densities, "near_list": near_list, "far_list": far_list, "far_class": far_class, "coarse_list": coarse_list, "coarse_class": coarse_class, "translations": translations, "check_to_equiv": check_to_equiv, "up_check_to_equiv": up_check_to_equiv, "partial_check": partial_check, "contrib_ids": contrib_ids}


soft_sq = 0.0625
surface_half = 2.5
grid_side = 32

def surface_points(surf_order):
    ladder = np.arange(surf_order)
    first, second, third = np.meshgrid(ladder, ladder, ladder, indexing='ij')
    last_index = surf_order - 1
    on_edge = (first == 0) | (first == last_index) | (second == 0) | (second == last_index) | (third == 0) | (third == last_index)
    coords = np.stack([first[on_edge], second[on_edge], third[on_edge]]).astype(np.float32)
    return jnp.asarray(-surface_half + 2.0 * surface_half * coords / last_index, jnp.float32)

def leaf_centres(leaf_ids):
    across = leaf_ids % grid_side
    along = leaf_ids // grid_side % grid_side
    upward = leaf_ids // (grid_side * grid_side)
    return 2.0 * jnp.stack([across, along, upward], axis=1).astype(jnp.float32)

def near_block(targets, neighbours):
    gap_first = targets[:, None, 0, :, None] - neighbours[:, :, 0, None, :]
    gap_second = targets[:, None, 1, :, None] - neighbours[:, :, 1, None, :]
    gap_third = targets[:, None, 2, :, None] - neighbours[:, :, 2, None, :]
    kernel = lax.rsqrt(gap_first * gap_first + gap_second * gap_second + gap_third * gap_third + soft_sq)
    return lax.optimization_barrier(jnp.sum(kernel * neighbours[:, :, 3, None, :], axis=(1, 3)))

def far_block(local_pos, equiv_rows, surface):
    gap_first = local_pos[:, 0, :, None] - surface[0][None, None, :]
    gap_second = local_pos[:, 1, :, None] - surface[1][None, None, :]
    gap_third = local_pos[:, 2, :, None] - surface[2][None, None, :]
    kernel = lax.rsqrt(gap_first * gap_first + gap_second * gap_second + gap_third * gap_third + soft_sq)
    return lax.optimization_barrier(jnp.sum(kernel * equiv_rows[:, None, :], axis=2))

def reference(sources, live_counts, densities, near_list, far_list, far_class, coarse_list, coarse_class, translations, check_to_equiv, up_check_to_equiv, partial_check, contrib_ids):
    highest = lax.Precision.HIGHEST
    leaf_total = sources.shape[0]
    leaf_pts = sources.shape[2]
    leaf_ids = jnp.arange(leaf_total, dtype=jnp.int32)
    centres = leaf_centres(leaf_ids)
    is_live = jnp.arange(leaf_pts, dtype=jnp.int32)[None, :] < live_counts[:, None]
    positions = sources[:, :3, :] + centres[:, :, None]
    charges = jnp.where(is_live, sources[:, 3, :], 0.0)
    packed = jnp.concatenate([positions, charges[:, None, :]], axis=1)
    step_leaves = 8
    blocks = leaf_total // step_leaves

    def near_step(inputs):
        targets, chosen = inputs
        return near_block(targets, packed[chosen])
    near_pot = lax.map(near_step, (positions.reshape(blocks, step_leaves, 3, leaf_pts), near_list.reshape(blocks, step_leaves, -1)))
    near_pot = near_pot.reshape(leaf_total, leaf_pts)
    owner_count = partial_check.shape[0]
    p_rows = partial_check.shape[1]
    slot_count = partial_check.shape[2]
    columns = jnp.transpose(partial_check, (0, 2, 1)).reshape(owner_count * slot_count, p_rows)
    summed = jax.ops.segment_sum(columns, contrib_ids.reshape(-1).astype(jnp.int32), num_segments=SHARED)
    up_check = summed.T
    up_equiv = jnp.dot(up_check_to_equiv, up_check, precision=highest, preferred_element_type=jnp.float32)
    class_ids = jnp.arange(translations.shape[0], dtype=jnp.int32)
    far_hot = (far_class[:, :, None] == class_ids[None, None, :]).astype(jnp.float32)
    coarse_hot = (coarse_class[:, :, None] == class_ids[None, None, :]).astype(jnp.float32)
    far_cols = densities[:, far_list]
    coarse_cols = up_equiv[:, coarse_list]
    gathered = jnp.einsum('ptf,tfc->cpt', far_cols, far_hot, precision=highest) + jnp.einsum('ptf,tfc->cpt', coarse_cols, coarse_hot, precision=highest)
    down_check = jnp.einsum('cpq,cqt->pt', translations, gathered, precision=highest)
    down_equiv = jnp.dot(check_to_equiv, down_check, precision=highest, preferred_element_type=jnp.float32)
    surface = surface_points(ORDER)
    far_leaves = 64
    far_blocks = leaf_total // far_leaves

    def far_step(inputs):
        local_pos, equiv_rows = inputs
        return far_block(local_pos, equiv_rows, surface)
    far_pot = lax.map(far_step, (sources[:, :3, :].reshape(far_blocks, far_leaves, 3, leaf_pts), down_equiv.T.reshape(far_blocks, far_leaves, -1)))
    far_pot = far_pot.reshape(leaf_total, leaf_pts)
    return jnp.where(is_live, near_pot + far_pot, 0.0)
```

```python
import math

import jax
import jax.numpy as jnp
import numpy as np
from jax import lax
from jax.experimental import pallas as pl
from jax.experimental.pallas import tpu as pltpu
from jax.sharding import PartitionSpec as P

ORDER = 8
SHARED = 1024


soft_sq = 0.0625
surface_half = 2.5
grid_side = 32


def surface_points(surf_order):
    ladder = np.arange(surf_order)
    first, second, third = np.meshgrid(ladder, ladder, ladder, indexing="ij")
    last_index = surf_order - 1
    on_edge = (
        (first == 0)
        | (first == last_index)
        | (second == 0)
        | (second == last_index)
        | (third == 0)
        | (third == last_index)
    )
    coords = np.stack([first[on_edge], second[on_edge], third[on_edge]]).astype(np.float32)
    return jnp.asarray(-surface_half + 2.0 * surface_half * coords / last_index, jnp.float32)


def leaf_centres(leaf_ids):
    across = leaf_ids % grid_side
    along = leaf_ids // grid_side % grid_side
    upward = leaf_ids // (grid_side * grid_side)
    return 2.0 * jnp.stack([across, along, upward], axis=1).astype(jnp.float32)


def near_block(targets, neighbours):
    gap_first = targets[:, None, 0, :, None] - neighbours[:, :, 0, None, :]
    gap_second = targets[:, None, 1, :, None] - neighbours[:, :, 1, None, :]
    gap_third = targets[:, None, 2, :, None] - neighbours[:, :, 2, None, :]
    kernel = lax.rsqrt(
        gap_first * gap_first + gap_second * gap_second + gap_third * gap_third + soft_sq
    )
    return jnp.sum(kernel * neighbours[:, :, 3, None, :], axis=(1, 3))


def far_block(local_pos, equiv_rows, surface):
    gap_first = local_pos[:, 0, :, None] - surface[0][None, None, :]
    gap_second = local_pos[:, 1, :, None] - surface[1][None, None, :]
    gap_third = local_pos[:, 2, :, None] - surface[2][None, None, :]
    kernel = lax.rsqrt(
        gap_first * gap_first + gap_second * gap_second + gap_third * gap_third + soft_sq
    )
    return jnp.sum(kernel * equiv_rows[:, None, :], axis=2)


MESH = pl.DeviceIdType.MESH


def up_kernel(ids_ref, part_ref, mat_ref, dens_ref, pack_ref, pv_ref, dw_ref, sw_ref, wt, rt, p0s, p0r, hs, hr, zs, zr, as_, ar, bs, br, fs, fr):
    highest = lax.Precision.HIGHEST
    z = lax.axis_index("gx")
    gy = lax.axis_index("gy")
    x, y, c = gy // 8, (gy // 2) % 4, gy % 2
    chip = z * 16 + x * 4 + y
    partner = (z, gy + 1 - 2 * c)
    a = x + c * (y - x)
    b = y + c * (x - y)

    def chip_dev(q, core):
        return (q // 16, ((q // 4) % 4) * 8 + (q % 4) * 2 + core)

    def ab_dev(a1, b1):
        return (z, (a1 + c * (b1 - a1)) * 8 + (b1 + c * (a1 - b1)) * 2 + c)

    prev_chip = (chip + 127) % 128
    next_chip = (chip + 1) % 128
    adj_chip = (chip + 127 + 2 * c) % 128

    barrier = pltpu.get_barrier_semaphore()
    peers = [partner, chip_dev(prev_chip, 1), chip_dev(next_chip, 0)]
    peers += [((z + k) % 8, gy) for k in range(1, 8)]
    peers += [ab_dev((a + k) % 4, b) for k in range(1, 4)]
    peers += [ab_dev(a, (b + k) % 4) for k in range(1, 4)]
    for peer in peers:
        pl.semaphore_signal(barrier, inc=1, device_id=peer, device_id_type=MESH)

    rows = lax.broadcasted_iota(jnp.int32, (16, 64), 0)
    adj_base = 8 * chip - 8 + 16 * c
    wanted = jnp.where(rows < 8, 8 * chip + rows, adj_base + rows - 8)
    hot = (wanted == ids_ref[...]).astype(jnp.float32)
    mine = jnp.dot(hot, part_ref[...], precision=highest, preferred_element_type=jnp.float32)
    mine = lax.dot_general(mine, mat_ref[...], (((1,), (1,)), ((), ())), precision=highest, preferred_element_type=jnp.float32)
    wt[...] = jnp.zeros_like(wt)
    wt[0, :, 0:296] = mine[0:8]
    wt[1, :, 0:296] = mine[8:16]

    pl.semaphore_wait(barrier, len(peers))

    def rcopy(src, dst, ssem, rsem, dev):
        return pltpu.make_async_remote_copy(src_ref=src, dst_ref=dst, send_sem=ssem, recv_sem=rsem, device_id=dev, device_id_type=MESH)

    sends = []

    def send(src, dst, ssem, rsem, dev):
        cp = rcopy(src, dst, ssem, rsem, dev)
        cp.start()
        sends.append(cp)

    send(wt.at[1], rt.at[2 - c], p0s.at[1], p0r.at[2 - c], chip_dev(adj_chip, 0))
    send(wt.at[1], rt.at[2 - c], p0s.at[2], p0r.at[2 - c], chip_dev(adj_chip, 1))
    send(wt.at[0], rt.at[0], p0s.at[0], p0r.at[0], partner)
    d = z * 32 + gy
    up_d, down_d = (d + 1) % 256, (d + 255) % 256
    up_dev, down_dev = (up_d // 32, up_d % 32), (down_d // 32, down_d % 32)
    send(pack_ref, sw_ref.at[0], hs.at[0], hr.at[0], up_dev)
    send(pack_ref, sw_ref.at[1], hs.at[1], hr.at[1], down_dev)
    send(dens_ref, dw_ref.at[0], hs.at[2], hr.at[2], up_dev)
    send(dens_ref, dw_ref.at[1], hs.at[3], hr.at[3], down_dev)

    def arrive(dst, rsem):
        rcopy(dst, dst, fs.at[0], rsem, partner).wait_recv()

    for k in range(3):
        arrive(rt.at[k], p0r.at[k])
    total = wt[0] + rt[0] + rt[1] + rt[2]
    tile = jnp.where(c == 0, total[:, 0:128], total[:, 128:256])
    tail = jnp.where(c == 0, total[0:4, 256:384], total[4:8, 256:384])
    pv_ref[c, b, a, z, 0] = tile[0:4]
    pv_ref[c, b, a, z, 1] = tile[4:8]
    pv_ref[c, b, a, z, 2] = tail

    for k in (4, 3, 5, 2, 6, 1, 7):
        spot = pv_ref.at[c, b, a, z]
        send(spot, spot, zs.at[k - 1], zr.at[k - 1], ((z + k) % 8, gy))
    for k in (1, 7, 2, 6, 3, 5, 4):
        arrive(pv_ref.at[c, b, a, (z + 8 - k) % 8], zr.at[k - 1])

    forwards = 0

    def forward(spot):
        nonlocal forwards
        send(spot, spot, fs.at[forwards], fr.at[forwards], partner)
        forwards += 1

    spot = pv_ref.at[c, b, a]
    for k in (2, 1, 3):
        send(spot, spot, as_.at[k - 1], ar.at[k - 1], ab_dev((a + k) % 4, b))
    for k in (2, 1, 3):
        send(spot, spot, bs.at[0, k - 1], br.at[0, k - 1], ab_dev(a, (b + k) % 4))
    forward(spot)
    for j in (1, 3, 2):
        spot = pv_ref.at[c, b, (a + 4 - j) % 4]
        arrive(spot, ar.at[j - 1])
        for k in (2, 1, 3):
            send(spot, spot, bs.at[j, k - 1], br.at[j, k - 1], ab_dev(a, (b + k) % 4))
        forward(spot)
    for j in (0, 1, 3, 2):
        for k in (1, 3, 2):
            spot = pv_ref.at[c, (b + 4 - k) % 4, (a + 4 - j) % 4]
            arrive(spot, br.at[j, k - 1])
            forward(spot)
    n = 0
    arrive(pv_ref.at[1 - c, a, b], fr.at[n])
    n += 1
    for j in (1, 3, 2):
        arrive(pv_ref.at[1 - c, a, (b + 4 - j) % 4], fr.at[n])
        n += 1
    for j in (0, 1, 3, 2):
        for k in (1, 3, 2):
            arrive(pv_ref.at[1 - c, (a + 4 - k) % 4, (b + 4 - j) % 4], fr.at[n])
            n += 1
    for k in range(2):
        arrive(sw_ref.at[k], hr.at[k])
        arrive(dw_ref.at[k], hr.at[2 + k])
    for cp in sends:
        cp.wait_send()


def exchange(contrib_ids, partial_t, up_matrix, dens_t, packed):
    vmem = pl.BlockSpec(memory_space=pltpu.VMEM)
    dma = pltpu.SemaphoreType.DMA
    return pl.pallas_call(
        up_kernel,
        out_shape=(
            jax.ShapeDtypeStruct((2, 4, 4, 8, 3, 4, 128), jnp.float32),
            jax.ShapeDtypeStruct((2, 32, 296), jnp.float32),
            jax.ShapeDtypeStruct((2, 32, 4, 256), jnp.float32),
        ),
        in_specs=[vmem] * 5,
        out_specs=(vmem, vmem, vmem),
        scratch_shapes=[
            pltpu.VMEM((2, 8, 384), jnp.float32),
            pltpu.VMEM((3, 8, 384), jnp.float32),
            dma((3,)), dma((3,)), dma((4,)), dma((4,)), dma((7,)), dma((7,)),
            dma((3,)), dma((3,)), dma((4, 3)), dma((4, 3)), dma((16,)), dma((16,)),
        ],
        compiler_params=pltpu.CompilerParams(collective_id=0, has_side_effects=True),
    )(contrib_ids, partial_t, up_matrix, dens_t, packed)


def on_device(
    sources,
    live_counts,
    densities,
    near_list,
    far_list,
    far_class,
    coarse_list,
    coarse_class,
    translations,
    check_to_equiv,
    up_check_to_equiv,
    partial_check,
    contrib_ids,
):
    highest = lax.Precision.HIGHEST
    own_leaves = sources.shape[0]
    leaf_pts = sources.shape[2]
    device = lax.axis_index(("gx", "gy"))
    first_leaf = device * own_leaves
    window_start = first_leaf - own_leaves
    leaf_ids = first_leaf + jnp.arange(own_leaves, dtype=jnp.int32)
    centres = leaf_centres(leaf_ids)
    is_live = jnp.arange(leaf_pts, dtype=jnp.int32)[None, :] < live_counts[:, None]
    positions = sources[:, :3, :] + centres[:, :, None]
    charges = jnp.where(is_live, sources[:, 3, :], 0.0)
    packed = jnp.concatenate([positions, charges[:, None, :]], axis=1)
    dens_t = densities.T
    pieces, dens_sides, near_sides = exchange(
        contrib_ids, partial_check[0].T, up_check_to_equiv, dens_t, packed
    )
    window = jnp.concatenate([near_sides[0], packed, near_sides[1]], axis=0)
    dens_window = jnp.concatenate([dens_sides[0], dens_t, dens_sides[1]], axis=0).T
    first = pieces[0]
    second = pieces[1].transpose(1, 0, 2, 3, 4, 5)
    block_a = first[:, :, :, 0:2].reshape(4, 4, 8, 8, 128)
    block_b = second[:, :, :, 0:2].reshape(4, 4, 8, 8, 128)
    block_c = jnp.concatenate([first[:, :, :, 2], second[:, :, :, 2]], axis=3)
    up_rows = jnp.concatenate([block_a, block_b, block_c], axis=4)
    up_rows = up_rows.transpose(2, 1, 0, 3, 4).reshape(SHARED, 384)[:, :296]
    up_equiv = up_rows.T
    near_local = near_list - window_start
    step_leaves = math.gcd(own_leaves, 8)
    blocks = own_leaves // step_leaves

    def near_step(inputs):
        targets, chosen = inputs
        return near_block(targets, window[chosen])

    near_pot = lax.map(
        near_step,
        (
            positions.reshape(blocks, step_leaves, 3, leaf_pts),
            near_local.reshape(blocks, step_leaves, -1),
        ),
    )
    near_pot = near_pot.reshape(own_leaves, leaf_pts)
    class_ids = jnp.arange(translations.shape[0], dtype=jnp.int32)
    far_hot = (far_class[:, :, None] == class_ids[None, None, :]).astype(jnp.float32)
    coarse_hot = (coarse_class[:, :, None] == class_ids[None, None, :]).astype(jnp.float32)
    far_cols = dens_window[:, far_list - window_start]
    coarse_cols = up_equiv[:, coarse_list]
    gathered = jnp.einsum("ptf,tfc->cpt", far_cols, far_hot, precision=highest) + jnp.einsum(
        "ptf,tfc->cpt", coarse_cols, coarse_hot, precision=highest
    )
    down_check = jnp.einsum("cpq,cqt->pt", translations, gathered, precision=highest)
    down_equiv = jnp.dot(
        check_to_equiv, down_check, precision=highest, preferred_element_type=jnp.float32
    )
    surface = surface_points(ORDER)
    far_leaves = math.gcd(own_leaves, 16)
    far_blocks = own_leaves // far_leaves

    def far_step(inputs):
        local_pos, equiv_rows = inputs
        return far_block(local_pos, equiv_rows, surface)

    far_pot = lax.map(
        far_step,
        (
            sources[:, :3, :].reshape(far_blocks, far_leaves, 3, leaf_pts),
            down_equiv.T.reshape(far_blocks, far_leaves, -1),
        ),
    )
    far_pot = far_pot.reshape(own_leaves, leaf_pts)
    return jnp.where(is_live, near_pot + far_pot, 0.0)


def solution(mesh):
    return jax.shard_map(
        on_device,
        mesh=mesh,
        in_specs=(
            P(("gx", "gy"), None, None),
            P(("gx", "gy")),
            P(None, ("gx", "gy")),
            P(("gx", "gy"), None),
            P(("gx", "gy"), None),
            P(("gx", "gy"), None),
            P(("gx", "gy"), None),
            P(("gx", "gy"), None),
            P(),
            P(),
            P(),
            P(("gx", "gy"), None, None),
            P(("gx", "gy"), None),
        ),
        out_specs=P(("gx", "gy"), None),
        check_vma=False,
    )
```

```python
import jax
import jax.numpy as jnp
import numpy as np
from jax import lax
from jax.experimental import pallas as pl
from jax.experimental.pallas import tpu as pltpu
from jax.sharding import PartitionSpec as P

MESH = pl.DeviceIdType.MESH
ORDER = 8
P_SIZE = 296
SOFT = 0.0625
HALF = 2.5
PARTS = 48
NEAR_SPLIT = (0, 8, 14, 32, 32)


def surface_rows():
    ladder = np.arange(ORDER)
    grid = np.stack(np.meshgrid(ladder, ladder, ladder, indexing="ij")).reshape(3, -1)
    grid = grid[:, ((grid == 0) | (grid == ORDER - 1)).any(axis=0)].astype(np.float32)
    return (-HALF + 2.0 * HALF * grid / (ORDER - 1)).astype(np.float32)


def two(v):
    high = v.astype(jnp.bfloat16).astype(jnp.float32)
    low = (v - high).astype(jnp.bfloat16).astype(jnp.float32)
    return high, low


def three(v):
    high, mid = two(v)
    return high, mid, (v - high - mid).astype(jnp.bfloat16).astype(jnp.float32)


def target_rows(v):
    high, low = two(v)
    seen = high + low
    one = jnp.ones_like(v)
    return (high, high, low, low, one, one, one) + three(seen * seen)


def source_rows(v):
    high, low = two(v)
    seen = high + low
    one = jnp.ones_like(v)
    return (-2.0 * high, -2.0 * low, -2.0 * high, -2.0 * low) + three(seen * seen) + (one, one, one)


def dot_t(a, b):
    return lax.dot_general(a, b, (((1,), (1,)), ((), ())), preferred_element_type=jnp.float32)


def dot_n(a, b):
    return jnp.dot(a, b, preferred_element_type=jnp.float32)


def halves(v):
    high = v.astype(jnp.bfloat16)
    return high, (v - high.astype(jnp.float32)).astype(jnp.bfloat16)


def fmm_kernel(
    near_ref, live_ref, src_hbm, dens_hbm, flist_hbm, fclass_hbm, clist_hbm, cclass_hbm, trans_hbm, down_hbm, up_hbm,
    part_hbm, ids_hbm, surf_hbm, out_ref,
    pv_ref, wt, rt, win, dw, flist, fclass, clist, cclass, trans, down, up, part, ids, surf,
    tfeat, fa, fb, qa, qb, th, tl, gfar, up_high, up_low, equiv, near_rows,
    p0s, p0r, hs, hr, zs, zr, as_, ar, bs, br, fs, fr, ls,
):
    highest = lax.Precision.HIGHEST
    z = lax.axis_index("gx")
    gy = lax.axis_index("gy")
    x, y, c = gy // 8, (gy // 2) % 4, gy % 2
    chip = z * 16 + x * 4 + y
    d = z * 32 + gy
    partner = (z, gy + 1 - 2 * c)
    a = x + c * (y - x)
    b = y + c * (x - y)

    def chip_dev(q, core):
        return (q // 16, ((q // 4) % 4) * 8 + (q % 4) * 2 + core)

    def ab_dev(a1, b1):
        return (z, (a1 + c * (b1 - a1)) * 8 + (b1 + c * (a1 - b1)) * 2 + c)

    prev_chip = (chip + 127) % 128
    next_chip = (chip + 1) % 128
    adj_chip = (chip + 127 + 2 * c) % 128

    barrier = pltpu.get_barrier_semaphore()
    peers = [partner, chip_dev(prev_chip, 1), chip_dev(next_chip, 0)]
    peers += [((z + k) % 8, gy) for k in (4, 3, 5, 2, 6, 1, 7)]
    peers += [ab_dev((a + k) % 4, b) for k in range(1, 4)]
    peers += [ab_dev(a, (b + k) % 4) for k in range(1, 4)]
    for peer in peers:
        pl.semaphore_signal(barrier, inc=1, device_id=peer, device_id_type=MESH)

    loads = [
        pltpu.make_async_copy(s, t, ls.at[i])
        for i, (s, t) in enumerate(
            (
                (ids_hbm, ids), (part_hbm, part), (up_hbm, up), (src_hbm, win.at[pl.ds(32, 32)]),
                (dens_hbm, dw.at[pl.ds(32, 32)]), (flist_hbm, flist), (fclass_hbm, fclass), (clist_hbm, clist),
                (cclass_hbm, cclass), (surf_hbm, surf), (down_hbm, down), (trans_hbm, trans),
            )
        )
    ]
    for load in loads:
        load.start()

    rows = lax.broadcasted_iota(jnp.int32, (16, 64), 0)
    adj_base = 8 * chip - 8 + 16 * c
    wanted = jnp.where(rows < 8, 8 * chip + rows, adj_base + rows - 8)
    wt[...] = jnp.zeros_like(wt)
    for load in loads[0:3]:
        load.wait()
    hot = (wanted == ids[...]).astype(jnp.float32)
    mine = jnp.dot(hot, part[...], precision=highest, preferred_element_type=jnp.float32)
    mine = lax.dot_general(
        mine, up[...], (((1,), (1,)), ((), ())), precision=highest, preferred_element_type=jnp.float32
    )
    wt[0, :, 0:P_SIZE] = mine[0:8]
    wt[1, :, 0:P_SIZE] = mine[8:16]
    loads[3].wait()
    spot_row = lax.broadcasted_iota(jnp.int32, (4, 256), 0)
    spot_lane = lax.broadcasted_iota(jnp.int32, (4, 256), 1)

    def mask_leaf(t, carry):
        v = win[32 + t]
        win[32 + t] = jnp.where((spot_row == 3) & (spot_lane >= live_ref[t]), 0.0, v)
        return carry

    lax.fori_loop(0, 32, mask_leaf, 0)

    pl.semaphore_wait(barrier, len(peers))

    def rcopy(src, dst, ssem, rsem, dev):
        return pltpu.make_async_remote_copy(
            src_ref=src, dst_ref=dst, send_sem=ssem, recv_sem=rsem, device_id=dev, device_id_type=MESH
        )

    sends = []

    def send(src, dst, ssem, rsem, dev):
        cp = rcopy(src, dst, ssem, rsem, dev)
        cp.start()
        sends.append(cp)

    def arrive(dst, rsem):
        rcopy(dst, dst, fs.at[0], rsem, partner).wait_recv()

    send(wt.at[1], rt.at[2 - c], p0s.at[1], p0r.at[2 - c], chip_dev(adj_chip, 0))
    send(wt.at[1], rt.at[2 - c], p0s.at[2], p0r.at[2 - c], chip_dev(adj_chip, 1))
    send(wt.at[0], rt.at[0], p0s.at[0], p0r.at[0], partner)
    up_d, down_d = (d + 1) % 256, (d + 255) % 256
    up_dev, down_dev = (up_d // 32, up_d % 32), (down_d // 32, down_d % 32)
    own = win.at[pl.ds(32, 32)]
    send(own, win.at[pl.ds(0, 32)], hs.at[0], hr.at[0], up_dev)
    send(own, win.at[pl.ds(64, 32)], hs.at[1], hr.at[1], down_dev)
    send(dens_hbm, dw.at[pl.ds(0, 32)], hs.at[2], hr.at[2], up_dev)
    send(dens_hbm, dw.at[pl.ds(64, 32)], hs.at[3], hr.at[3], down_dev)

    def target_step(t, carry):
        v = jnp.where(spot_row < 3, win[32 + t], 0.0)
        for i, piece in enumerate(target_rows(v)):
            fa[4 * i : 4 * i + 4, 0:256] = piece
        tfeat[t] = jnp.transpose(fa[:, 0:256]).astype(jnp.bfloat16)
        return carry

    fa[40:PARTS, :] = jnp.zeros((PARTS - 40, 1024), jnp.float32)
    fb[40:PARTS, :] = jnp.zeros((PARTS - 40, 1024), jnp.float32)
    lax.fori_loop(0, 32, target_step, 0)

    for k in range(3):
        arrive(rt.at[k], p0r.at[k])
    total = wt[0] + rt[0] + rt[1] + rt[2]
    tile = jnp.where(c == 0, total[:, 0:128], total[:, 128:256])
    tail = jnp.where(c == 0, total[0:4, 256:384], total[4:8, 256:384])
    pv_ref[c, b, a, z, 0] = tile[0:4]
    pv_ref[c, b, a, z, 1] = tile[4:8]
    pv_ref[c, b, a, z, 2] = tail
    for k in (4, 3, 5, 2, 6, 1, 7):
        spot = pv_ref.at[c, b, a, z]
        send(spot, spot, zs.at[k - 1], zr.at[k - 1], ((z + k) % 8, gy))

    def prepare(t, feat, charge):
        for n in range(4):
            leaf = near_ref[n, t]
            v = win[jnp.clip(leaf - 32 * d + 32, 0, 95)]
            gap = jnp.where(spot_row == 0, leaf % 32 - t, 0)
            gap = jnp.where(spot_row == 1, (leaf // 32) % 32 - d % 32, gap)
            gap = jnp.where(spot_row == 2, leaf // 1024 - d // 32, gap)
            placed = jnp.where(spot_row < 3, v + 2.0 * gap.astype(jnp.float32), SOFT**0.5)
            for i, piece in enumerate(source_rows(placed)):
                feat[4 * i : 4 * i + 4, 256 * n : 256 * n + 256] = piece
            charge[0:1, 256 * n : 256 * n + 256] = v[3:4]

    def weigh(points, others, weights):
        count = others.shape[1]
        sums = []
        for i in range(0, 256, 64):
            pulled = lax.rsqrt(dot_n(points[i : i + 64], others)) * weights
            acc = pulled[:, 0:128]
            for j in range(128, count, 128):
                acc = acc + pulled[:, j : j + 128]
            sums.append(acc)
        return jnp.sum(jnp.transpose(jnp.concatenate(sums, axis=0)), axis=0, keepdims=True)

    def near_leaf(t, feat, charge):
        near_rows[pl.ds(t, 1), :] = weigh(tfeat[t], feat[...].astype(jnp.bfloat16), charge[0:1, :])

    def near_pair(i, carry):
        t = 2 * i
        prepare(t + 1, fb, qb)
        near_leaf(t, fa, qa)
        prepare(jnp.minimum(t + 2, 31), fa, qa)
        near_leaf(t + 1, fb, qb)
        return carry

    def near_part(k):
        if NEAR_SPLIT[k] < NEAR_SPLIT[k + 1]:
            lax.fori_loop(NEAR_SPLIT[k] // 2, NEAR_SPLIT[k + 1] // 2, near_pair, 0)

    for k in range(2):
        arrive(win.at[pl.ds(64 * k, 32)], hr.at[k])
    prepare(0, fa, qa)
    near_part(0)

    for k in (1, 7, 2, 6, 3, 5, 4):
        arrive(pv_ref.at[c, b, a, (z + 8 - k) % 8], zr.at[k - 1])
    forwards = 0

    def forward(spot):
        nonlocal forwards
        send(spot, spot, fs.at[forwards], fr.at[forwards], partner)
        forwards += 1

    spot = pv_ref.at[c, b, a]
    for k in (2, 1, 3):
        send(spot, spot, as_.at[k - 1], ar.at[k - 1], ab_dev((a + k) % 4, b))
    for k in (2, 1, 3):
        send(spot, spot, bs.at[0, k - 1], br.at[0, k - 1], ab_dev(a, (b + k) % 4))
    forward(spot)

    near_part(1)

    for j in (1, 3, 2):
        spot = pv_ref.at[c, b, (a + 4 - j) % 4]
        arrive(spot, ar.at[j - 1])
        for k in (2, 1, 3):
            send(spot, spot, bs.at[j, k - 1], br.at[j, k - 1], ab_dev(a, (b + k) % 4))
        forward(spot)

    for load in loads[4:]:
        load.wait()

    def split_step(i, carry):
        th[i], tl[i] = halves(trans[i])
        return carry

    lax.fori_loop(0, 16, split_step, 0)
    near_part(2)

    for k in range(2):
        arrive(dw.at[pl.ds(64 * k, 32)], hr.at[2 + k])

    def columns(ref):
        return jnp.transpose(ref[...])

    def choose(cols, count, width):
        lane = lax.broadcasted_iota(jnp.int32, (32, width), 1)
        return jnp.concatenate(
            [(cols[:, k : k + 1] == lane).astype(jnp.float32) for k in range(count)], axis=0
        ).astype(jnp.bfloat16)

    def by_class(ref, count):
        table = ref[...]
        pad = jnp.zeros((count, 96), jnp.int32)
        wide = jnp.concatenate([table, pad], axis=1)
        tiles = []
        for k in range(0, count, 4):
            row = wide[k : k + 1]
            for m in range(1, 4):
                row = row + pltpu.roll(wide[k + m : k + m + 1], 32 * m, 1)
            tiles.append(row)
        row = jnp.concatenate(tiles, axis=1)
        shape = (512, 32 * count)
        line = lax.broadcasted_iota(jnp.int32, shape, 0)
        lane = lax.broadcasted_iota(jnp.int32, shape, 1)
        code = row * 32 + lax.broadcasted_iota(jnp.int32, row.shape, 1) % 32
        return jnp.where(code == line, 1.0, 0.0).astype(jnp.bfloat16)

    far_pick = choose(columns(flist) - 32 * d + 32, 16, 96)
    dens_high, dens_low = halves(dw[...])
    far_high = dot_n(far_pick, dens_high).astype(jnp.bfloat16)
    far_low = dot_n(far_pick, dens_low).astype(jnp.bfloat16)
    far_class = by_class(fclass, 16)
    gfar[...] = dot_n(far_class, far_high) + dot_n(far_class, far_low)

    near_part(3)

    for j in (0, 1, 3, 2):
        for k in (1, 3, 2):
            spot = pv_ref.at[c, (b + 4 - k) % 4, (a + 4 - j) % 4]
            arrive(spot, br.at[j, k - 1])
            forward(spot)

    coarse_pick = choose(columns(clist), 8, 1024)
    coarse_class = by_class(cclass, 8)
    down_high, down_low = halves(down[...])

    n = 0
    arrive(pv_ref.at[1 - c, a, b], fr.at[n])
    n += 1
    for j in (1, 3, 2):
        arrive(pv_ref.at[1 - c, a, (b + 4 - j) % 4], fr.at[n])
        n += 1
    for j in (0, 1, 3, 2):
        for k in (1, 3, 2):
            arrive(pv_ref.at[1 - c, (a + 4 - k) % 4, (b + 4 - j) % 4], fr.at[n])
            n += 1

    def collect(i, carry):
        zz, xx, yy = i // 8, (i // 2) % 4, (i % 2) * 2
        parts = []
        for q in range(2):
            one, two_ = pv_ref[0, yy + q, xx, zz], pv_ref[1, xx, yy + q, zz]
            parts.append(
                jnp.concatenate(
                    [
                        jnp.concatenate([one[0], one[1]], axis=0),
                        jnp.concatenate([two_[0], two_[1]], axis=0),
                        jnp.concatenate([one[2], two_[2]], axis=0),
                    ],
                    axis=1,
                )
            )
        high, low = halves(jnp.concatenate(parts, axis=0))
        up_high[pl.ds(pl.multiple_of(16 * i, 16), 16), :] = high
        up_low[pl.ds(pl.multiple_of(16 * i, 16), 16), :] = low
        return carry

    lax.fori_loop(0, 64, collect, 0, unroll=8)
    coarse_high = dot_n(coarse_pick, up_high[...]).astype(jnp.bfloat16)
    coarse_low = dot_n(coarse_pick, up_low[...]).astype(jnp.bfloat16)
    gathered = gfar[...] + (dot_n(coarse_class, coarse_high) + dot_n(coarse_class, coarse_low))[:, 0:P_SIZE]
    g_high, g_low = halves(gathered)
    wide_sum = jnp.zeros((P_SIZE, 64), jnp.float32)
    slim_sum = jnp.zeros((P_SIZE, 32), jnp.float32)
    for i in range(16):
        high, low = g_high[32 * i : 32 * i + 32], g_low[32 * i : 32 * i + 32]
        wide_sum = wide_sum + dot_t(th[i], jnp.concatenate([high, low], axis=0))
        slim_sum = slim_sum + dot_t(tl[i], high)
    check = wide_sum[:, 0:32] + wide_sum[:, 32:64] + slim_sum
    c_high, c_low = halves(jnp.transpose(check))
    equiv[...] = jnp.zeros_like(equiv)
    equiv[:, 0:P_SIZE] = dot_t(c_high, down_high) + dot_t(c_low, down_high) + dot_t(c_high, down_low)

    out_lane = lax.broadcasted_iota(jnp.int32, (1, 256), 1)
    far_points = surf[...]

    def far_leaf(t, carry):
        row = near_rows[pl.ds(t, 1), :] + weigh(tfeat[t], far_points, equiv[pl.ds(t, 1), :])
        out_ref[pl.ds(t, 1), :] = jnp.where(out_lane < live_ref[t], row, 0.0)
        return carry

    lax.fori_loop(0, 32, far_leaf, 0, unroll=2)
    for cp in sends:
        cp.wait_send()


def surface_features():
    points = np.zeros((4, 384), np.float32)
    points[:3, :P_SIZE] = surface_rows()
    points[3, :] = SOFT**0.5
    points[:3, P_SIZE:] = HALF

    def short(v):
        return v.astype(jnp.bfloat16).astype(np.float32)

    high = short(points)
    low = short(points - high)
    seen = high + low
    square = seen * seen
    s1 = short(square)
    s2 = short(square - s1)
    s3 = short(square - s1 - s2)
    one = np.ones_like(points)
    rows = [-2 * high, -2 * low, -2 * high, -2 * low, s1, s2, s3, one, one, one]
    stacked = np.concatenate(rows + [np.zeros((PARTS - 40, 384), np.float32)], axis=0)
    return stacked.astype(jnp.bfloat16)


def on_device(
    sources, live_counts, densities, near_list, far_list, far_class, coarse_list, coarse_class, translations,
    check_to_equiv, up_check_to_equiv, partial_check, contrib_ids,
):
    smem = pl.BlockSpec(memory_space=pltpu.SMEM)
    hbm = pl.BlockSpec(memory_space=pl.ANY)
    vmem = pl.BlockSpec(memory_space=pltpu.VMEM)
    dma = pltpu.SemaphoreType.DMA
    f32, bf16, i32 = jnp.float32, jnp.bfloat16, jnp.int32
    return pl.pallas_call(
        fmm_kernel,
        out_shape=jax.ShapeDtypeStruct((32, 256), f32),
        in_specs=[smem, smem] + [hbm] * 12,
        out_specs=vmem,
        scratch_shapes=[
            pltpu.VMEM((2, 4, 4, 8, 3, 4, 128), f32),
            pltpu.VMEM((2, 8, 384), f32),
            pltpu.VMEM((3, 8, 384), f32),
            pltpu.VMEM((96, 4, 256), f32),
            pltpu.VMEM((96, P_SIZE), f32),
            pltpu.VMEM((16, 32), i32),
            pltpu.VMEM((16, 32), i32),
            pltpu.VMEM((8, 32), i32),
            pltpu.VMEM((8, 32), i32),
            pltpu.VMEM((16, P_SIZE, P_SIZE), f32),
            pltpu.VMEM((P_SIZE, P_SIZE), f32),
            pltpu.VMEM((P_SIZE, P_SIZE), f32),
            pltpu.VMEM((64, P_SIZE), f32),
            pltpu.VMEM((1, 64), i32),
            pltpu.VMEM((PARTS, 384), bf16),
            pltpu.VMEM((32, 256, PARTS), bf16),
            pltpu.VMEM((PARTS, 1024), f32),
            pltpu.VMEM((PARTS, 1024), f32),
            pltpu.VMEM((8, 1024), f32),
            pltpu.VMEM((8, 1024), f32),
            pltpu.VMEM((16, P_SIZE, P_SIZE), bf16),
            pltpu.VMEM((16, P_SIZE, P_SIZE), bf16),
            pltpu.VMEM((512, P_SIZE), f32),
            pltpu.VMEM((1024, 384), bf16),
            pltpu.VMEM((1024, 384), bf16),
            pltpu.VMEM((32, 384), f32),
            pltpu.VMEM((32, 256), f32),
            dma((3,)), dma((3,)), dma((4,)), dma((4,)), dma((7,)), dma((7,)),
            dma((3,)), dma((3,)), dma((4, 3)), dma((4, 3)), dma((16,)), dma((16,)), dma((12,)),
        ],
        compiler_params=pltpu.CompilerParams(
            collective_id=0, has_side_effects=True, vmem_limit_bytes=60 * 1024 * 1024
        ),
    )(
        near_list.T, live_counts, sources, densities.T, far_list.T, far_class.T, coarse_list.T, coarse_class.T,
        translations, check_to_equiv, up_check_to_equiv, partial_check[0].T, contrib_ids,
        jnp.asarray(surface_features()),
    )


def solution(mesh):
    both = ("gx", "gy")
    return jax.shard_map(
        on_device,
        mesh=mesh,
        in_specs=(
            P(both, None, None), P(both), P(None, both), P(both, None), P(both, None), P(both, None), P(both, None),
            P(both, None), P(), P(), P(), P(both, None, None), P(both, None),
        ),
        out_specs=P(both, None),
        check_vma=False,
    )
```

```python
import jax
import jax.numpy as jnp
import numpy as np
from jax import lax
from jax.experimental import pallas as pl
from jax.experimental.pallas import tpu as pltpu
from jax.sharding import PartitionSpec as P

MESH = pl.DeviceIdType.MESH
ORDER = 8
P_SIZE = 296
SOFT = 0.0625
HALF = 2.5
PARTS = 48
NEAR_SPLIT = (0, 8, 16, 20, 24, 28, 32)


def surface_rows():
    ladder = np.arange(ORDER)
    grid = np.stack(np.meshgrid(ladder, ladder, ladder, indexing="ij")).reshape(3, -1)
    grid = grid[:, ((grid == 0) | (grid == ORDER - 1)).any(axis=0)].astype(np.float32)
    return (-HALF + 2.0 * HALF * grid / (ORDER - 1)).astype(np.float32)


def two(v):
    high = v.astype(jnp.bfloat16).astype(jnp.float32)
    low = (v - high).astype(jnp.bfloat16).astype(jnp.float32)
    return high, low


def three(v):
    high, mid = two(v)
    return high, mid, (v - high - mid).astype(jnp.bfloat16).astype(jnp.float32)


def target_rows(v):
    high, low = two(v)
    seen = high + low
    one = jnp.ones_like(v)
    return (high, high, low, low, one, one, one) + three(seen * seen)


def source_rows(v):
    high, low = two(v)
    seen = high + low
    one = jnp.ones_like(v)
    return (-2.0 * high, -2.0 * low, -2.0 * high, -2.0 * low) + three(seen * seen) + (one, one, one)


def dot_t(a, b):
    return lax.dot_general(a, b, (((1,), (1,)), ((), ())), preferred_element_type=jnp.float32)


def dot_n(a, b):
    return jnp.dot(a, b, preferred_element_type=jnp.float32)


def halves(v):
    high = v.astype(jnp.bfloat16)
    return high, (v - high.astype(jnp.float32)).astype(jnp.bfloat16)


def fmm_kernel(
    near_ref, live_ref, src_hbm, dens_hbm, flist_hbm, fclass_hbm, clist_hbm, cclass_hbm, trans_hbm, down_hbm, up_hbm,
    part_hbm, ids_hbm, surf_hbm, out_ref,
    pv_ref, wt, rt, win, dw, flist, fclass, clist, cclass, trans, down, up, part, ids, surf,
    tfeat, tfar, fa, fb, qa, qb, th, tl, gfar, up_high, up_low, pulls, near_rows,
    p0s, p0r, hs, hr, zs, zr, as_, ar, bs, br, fs, fr, ls,
):
    highest = lax.Precision.HIGHEST
    z = lax.axis_index("gx")
    gy = lax.axis_index("gy")
    x, y, c = gy // 8, (gy // 2) % 4, gy % 2
    chip = z * 16 + x * 4 + y
    d = z * 32 + gy
    partner = (z, gy + 1 - 2 * c)
    a = x + c * (y - x)
    b = y + c * (x - y)

    def chip_dev(q, core):
        return (q // 16, ((q // 4) % 4) * 8 + (q % 4) * 2 + core)

    def ab_dev(a1, b1):
        return (z, (a1 + c * (b1 - a1)) * 8 + (b1 + c * (a1 - b1)) * 2 + c)

    prev_chip = (chip + 127) % 128
    next_chip = (chip + 1) % 128
    adj_chip = (chip + 127 + 2 * c) % 128

    barrier = pltpu.get_barrier_semaphore()
    peers = [partner, chip_dev(prev_chip, 1), chip_dev(next_chip, 0)]
    peers += [((z + k) % 8, gy) for k in (4, 3, 5, 2, 6, 1, 7)]
    peers += [ab_dev((a + k) % 4, b) for k in range(1, 4)]
    peers += [ab_dev(a, (b + k) % 4) for k in range(1, 4)]
    for peer in peers:
        pl.semaphore_signal(barrier, inc=1, device_id=peer, device_id_type=MESH)

    loads = [
        pltpu.make_async_copy(s, t, ls.at[i])
        for i, (s, t) in enumerate(
            (
                (ids_hbm, ids), (part_hbm, part), (up_hbm, up), (src_hbm, win.at[pl.ds(32, 32)]),
                (dens_hbm, dw.at[pl.ds(32, 32)]), (flist_hbm, flist), (fclass_hbm, fclass), (clist_hbm, clist),
                (cclass_hbm, cclass), (surf_hbm, surf), (down_hbm, down), (trans_hbm, trans),
            )
        )
    ]
    for load in loads:
        load.start()

    rows = lax.broadcasted_iota(jnp.int32, (16, 64), 0)
    adj_base = 8 * chip - 8 + 16 * c
    wanted = jnp.where(rows < 8, 8 * chip + rows, adj_base + rows - 8)
    wt[...] = jnp.zeros_like(wt)
    for load in loads[0:3]:
        load.wait()
    hot = (wanted == ids[...]).astype(jnp.float32)
    mine = jnp.dot(hot, part[...], precision=highest, preferred_element_type=jnp.float32)
    mine = lax.dot_general(
        mine, up[...], (((1,), (1,)), ((), ())), precision=highest, preferred_element_type=jnp.float32
    )
    wt[0, :, 0:P_SIZE] = mine[0:8]
    wt[1, :, 0:P_SIZE] = mine[8:16]
    loads[3].wait()
    spot_row = lax.broadcasted_iota(jnp.int32, (4, 256), 0)
    spot_lane = lax.broadcasted_iota(jnp.int32, (4, 256), 1)

    def mask_leaf(t, carry):
        v = win[32 + t]
        win[32 + t] = jnp.where((spot_row == 3) & (spot_lane >= live_ref[t]), 0.0, v)
        return carry

    lax.fori_loop(0, 32, mask_leaf, 0)

    pl.semaphore_wait(barrier, len(peers))

    def rcopy(src, dst, ssem, rsem, dev):
        return pltpu.make_async_remote_copy(
            src_ref=src, dst_ref=dst, send_sem=ssem, recv_sem=rsem, device_id=dev, device_id_type=MESH
        )

    sends = []

    def send(src, dst, ssem, rsem, dev):
        cp = rcopy(src, dst, ssem, rsem, dev)
        cp.start()
        sends.append(cp)

    def arrive(dst, rsem):
        rcopy(dst, dst, fs.at[0], rsem, partner).wait_recv()

    send(wt.at[1], rt.at[2 - c], p0s.at[1], p0r.at[2 - c], chip_dev(adj_chip, 0))
    send(wt.at[1], rt.at[2 - c], p0s.at[2], p0r.at[2 - c], chip_dev(adj_chip, 1))
    send(wt.at[0], rt.at[0], p0s.at[0], p0r.at[0], partner)
    up_d, down_d = (d + 1) % 256, (d + 255) % 256
    up_dev, down_dev = (up_d // 32, up_d % 32), (down_d // 32, down_d % 32)
    own = win.at[pl.ds(32, 32)]
    send(own, win.at[pl.ds(0, 32)], hs.at[0], hr.at[0], up_dev)
    send(own, win.at[pl.ds(64, 32)], hs.at[1], hr.at[1], down_dev)
    send(dens_hbm, dw.at[pl.ds(0, 32)], hs.at[2], hr.at[2], up_dev)
    send(dens_hbm, dw.at[pl.ds(64, 32)], hs.at[3], hr.at[3], down_dev)

    def target_step(t, carry):
        v = jnp.where(spot_row < 3, win[32 + t], 0.0)
        for i, piece in enumerate(target_rows(v)):
            fa[4 * i : 4 * i + 4, 0:256] = piece
        tfeat[t] = jnp.transpose(fa[:, 0:256]).astype(jnp.bfloat16)
        tfar[t] = fa[:, 0:256].astype(jnp.bfloat16)
        return carry

    fa[40:PARTS, :] = jnp.zeros((PARTS - 40, 1024), jnp.float32)
    fb[40:PARTS, :] = jnp.zeros((PARTS - 40, 1024), jnp.float32)
    lax.fori_loop(0, 32, target_step, 0, unroll=4)
    loads[9].wait()
    far_points = surf

    def pull_step(t, carry):
        pulls[t] = lax.rsqrt(dot_n(far_points[...], tfar[t]))
        return carry

    lax.fori_loop(0, 32, pull_step, 0, unroll=8)

    for k in range(3):
        arrive(rt.at[k], p0r.at[k])
    total = wt[0] + rt[0] + rt[1] + rt[2]
    tile = jnp.where(c == 0, total[:, 0:128], total[:, 128:256])
    tail = jnp.where(c == 0, total[0:4, 256:384], total[4:8, 256:384])
    pv_ref[c, b, a, z, 0] = tile[0:4]
    pv_ref[c, b, a, z, 1] = tile[4:8]
    pv_ref[c, b, a, z, 2] = tail
    for k in (4, 3, 5, 2, 6, 1, 7):
        spot = pv_ref.at[c, b, a, z]
        send(spot, spot, zs.at[k - 1], zr.at[k - 1], ((z + k) % 8, gy))

    def prepare(t, feat, charge):
        for n in range(4):
            leaf = near_ref[n, t]
            v = win[jnp.clip(leaf - 32 * d + 32, 0, 95)]
            gap = jnp.where(spot_row == 0, leaf % 32 - t, 0)
            gap = jnp.where(spot_row == 1, (leaf // 32) % 32 - d % 32, gap)
            gap = jnp.where(spot_row == 2, leaf // 1024 - d // 32, gap)
            placed = jnp.where(spot_row < 3, v + 2.0 * gap.astype(jnp.float32), SOFT**0.5)
            for i, piece in enumerate(source_rows(placed)):
                feat[4 * i : 4 * i + 4, 256 * n : 256 * n + 256] = piece
            charge[0:1, 256 * n : 256 * n + 256] = v[3:4]

    def weigh(points, others, weights):
        count = others.shape[1]
        sums = []
        for i in range(0, 256, 64):
            pulled = lax.rsqrt(dot_n(points[i : i + 64], others)) * weights
            acc = pulled[:, 0:128]
            for j in range(128, count, 128):
                acc = acc + pulled[:, j : j + 128]
            sums.append(acc)
        return jnp.sum(jnp.transpose(jnp.concatenate(sums, axis=0)), axis=0, keepdims=True)

    def near_leaf(t, feat, charge):
        near_rows[pl.ds(t, 1), :] = weigh(tfeat[t], feat[...].astype(jnp.bfloat16), charge[0:1, :])

    def near_pair(i, carry):
        t = 2 * i
        prepare(t + 1, fb, qb)
        near_leaf(t, fa, qa)
        prepare(jnp.minimum(t + 2, 31), fa, qa)
        near_leaf(t + 1, fb, qb)
        return carry

    def near_part(k):
        if NEAR_SPLIT[k] < NEAR_SPLIT[k + 1]:
            lax.fori_loop(NEAR_SPLIT[k] // 2, NEAR_SPLIT[k + 1] // 2, near_pair, 0, unroll=2)

    for load in loads[4:9] + loads[10:]:
        load.wait()

    def split_step(i, carry):
        v = trans[i]
        at = pl.ds(pl.multiple_of(256 * i, 256), 256)
        th[:, at], tl[:, at] = halves(v[:, 0:256])
        return carry

    lax.fori_loop(0, 16, split_step, 0, unroll=2)
    lane = lax.broadcasted_iota(jnp.int32, (P_SIZE, 128), 1)
    blank = jnp.zeros((P_SIZE, 88), jnp.float32)
    for i in range(0, 16, 3):
        packed = jnp.zeros((P_SIZE, 128), jnp.float32)
        for m in range(min(3, 16 - i)):
            piece = jnp.concatenate([trans[i + m, :, 256:P_SIZE], blank], axis=1)
            packed = packed + (pltpu.roll(piece, 40 * m, 1) if m else piece)
        at = 4096 + 128 * (i // 3)
        th[:, at : at + 128], tl[:, at : at + 128] = halves(packed)
    for k in range(2):
        arrive(win.at[pl.ds(64 * k, 32)], hr.at[k])
    prepare(0, fa, qa)
    near_part(0)

    for k in (1, 7, 2, 6, 3, 5, 4):
        arrive(pv_ref.at[c, b, a, (z + 8 - k) % 8], zr.at[k - 1])
    forwards = 0

    def forward(spot):
        nonlocal forwards
        send(spot, spot, fs.at[forwards], fr.at[forwards], partner)
        forwards += 1

    spot = pv_ref.at[c, b, a]
    for k in (2, 1, 3):
        send(spot, spot, as_.at[k - 1], ar.at[k - 1], ab_dev((a + k) % 4, b))
    for k in (1, 3):
        send(spot, spot, bs.at[0, k - 1], br.at[0, k - 1], ab_dev(a, (b + k) % 4))
    forward(spot)

    near_part(1)

    for j in (1, 3, 2):
        spot = pv_ref.at[c, b, (a + 4 - j) % 4]
        arrive(spot, ar.at[j - 1])
        for k in (1, 3):
            send(spot, spot, bs.at[j, k - 1], br.at[j, k - 1], ab_dev(a, (b + k) % 4))
        forward(spot)

    def b_step(j):
        for k in (1, 3):
            spot = pv_ref.at[c, (b + 4 - k) % 4, (a + 4 - j) % 4]
            arrive(spot, br.at[j, k - 1])
            if (j in (0, 3)) == (k == 1):
                send(spot, spot, bs.at[j, 1], br.at[j, 1], ab_dev(a, (b + k) % 4))
            forward(spot)

    near_part(2)
    b_step(0)
    near_part(3)
    b_step(1)
    near_part(4)
    b_step(3)
    near_part(5)
    b_step(2)
    for k in range(2):
        arrive(dw.at[pl.ds(64 * k, 32)], hr.at[2 + k])

    def columns(ref):
        return jnp.transpose(ref[...])

    def choose(cols, count, width):
        lane = lax.broadcasted_iota(jnp.int32, (32, width), 1)
        return jnp.concatenate(
            [(cols[:, k : k + 1] == lane).astype(jnp.float32) for k in range(count)], axis=0
        ).astype(jnp.bfloat16)

    def by_class(ref, count):
        table = ref[...]
        pad = jnp.zeros((count, 96), jnp.int32)
        wide = jnp.concatenate([table, pad], axis=1)
        tiles = []
        for k in range(0, count, 4):
            row = wide[k : k + 1]
            for m in range(1, 4):
                row = row + pltpu.roll(wide[k + m : k + m + 1], 32 * m, 1)
            tiles.append(row)
        row = jnp.concatenate(tiles, axis=1)
        shape = (512, 32 * count)
        line = lax.broadcasted_iota(jnp.int32, shape, 0)
        lane = lax.broadcasted_iota(jnp.int32, shape, 1)
        code = row * 32 + lax.broadcasted_iota(jnp.int32, row.shape, 1) % 32
        return jnp.where(code == line, 1.0, 0.0).astype(jnp.bfloat16)

    far_pick = choose(columns(flist) - 32 * d + 32, 16, 96)
    dens_high, dens_low = halves(dw[...])
    far_high = dot_n(far_pick, dens_high).astype(jnp.bfloat16)
    far_low = dot_n(far_pick, dens_low).astype(jnp.bfloat16)
    far_class = by_class(fclass, 16)
    gfar[...] = jnp.zeros_like(gfar)
    gfar[:, 0:P_SIZE] = dot_n(far_class, far_high) + dot_n(far_class, far_low)

    coarse_pick = choose(columns(clist), 8, 1024)
    coarse_class = by_class(cclass, 8)
    down_high, down_low = halves(down[...])

    for j in (0, 1, 3, 2):
        spot = pv_ref.at[c, (b + 2) % 4, (a + 4 - j) % 4]
        arrive(spot, br.at[j, 1])
        forward(spot)

    n = 0
    arrive(pv_ref.at[1 - c, a, b], fr.at[n])
    n += 1
    for j in (1, 3, 2):
        arrive(pv_ref.at[1 - c, a, (b + 4 - j) % 4], fr.at[n])
        n += 1
    for j in (0, 1, 3, 2):
        for k in (1, 3):
            arrive(pv_ref.at[1 - c, (a + 4 - k) % 4, (b + 4 - j) % 4], fr.at[n])
            n += 1
    for j in (0, 1, 3, 2):
        arrive(pv_ref.at[1 - c, (a + 2) % 4, (b + 4 - j) % 4], fr.at[n])
        n += 1

    def collect(i, carry):
        zz, xx, yy = i // 8, (i // 2) % 4, (i % 2) * 2
        parts = []
        for q in range(2):
            one, two_ = pv_ref[0, yy + q, xx, zz], pv_ref[1, xx, yy + q, zz]
            parts.append(
                jnp.concatenate(
                    [
                        jnp.concatenate([one[0], one[1]], axis=0),
                        jnp.concatenate([two_[0], two_[1]], axis=0),
                        jnp.concatenate([one[2], two_[2]], axis=0),
                    ],
                    axis=1,
                )
            )
        high, low = halves(jnp.concatenate(parts, axis=0))
        up_high[pl.ds(pl.multiple_of(16 * i, 16), 16), :] = high
        up_low[pl.ds(pl.multiple_of(16 * i, 16), 16), :] = low
        return carry

    lax.fori_loop(0, 64, collect, 0, unroll=8)
    coarse_high = dot_n(coarse_pick, up_high[...]).astype(jnp.bfloat16)
    coarse_low = dot_n(coarse_pick, up_low[...]).astype(jnp.bfloat16)
    gathered = gfar[...] + dot_n(coarse_class, coarse_high) + dot_n(coarse_class, coarse_low)
    ends = []
    for i in range(0, 16, 3):
        packed = gathered[32 * i : 32 * i + 32, 256:384]
        for m in range(1, min(3, 16 - i)):
            packed = packed + pltpu.roll(gathered[32 * (i + m) : 32 * (i + m) + 32, 256:384], 40 * m, 1)
        ends.append(packed)
    spread = jnp.concatenate([gathered[32 * i : 32 * i + 32, 0:256] for i in range(16)] + ends, axis=1)
    g_high, g_low = halves(spread)
    wide_sum = dot_t(th[...], jnp.concatenate([g_high, g_low], axis=0))
    check = wide_sum[:, 0:32] + wide_sum[:, 32:64] + dot_t(tl[...], g_high)
    c_high, c_low = halves(check)
    equiv = dot_n(down_high, c_high) + dot_n(down_high, c_low) + dot_n(down_low, c_high)
    for t in range(32):
        far = jnp.sum(equiv[:, t : t + 1] * pulls[t], axis=0, keepdims=True)
        out_ref[t : t + 1, :] = near_rows[t : t + 1, :] + far
    for cp in sends:
        cp.wait_send()


def surface_features():
    points = np.concatenate([surface_rows(), np.full((1, P_SIZE), SOFT**0.5, np.float32)], axis=0)

    def short(v):
        return v.astype(jnp.bfloat16).astype(np.float32)

    high = short(points)
    low = short(points - high)
    seen = high + low
    square = seen * seen
    s1 = short(square)
    s2 = short(square - s1)
    s3 = short(square - s1 - s2)
    one = np.ones_like(points)
    rows = [-2 * high, -2 * low, -2 * high, -2 * low, s1, s2, s3, one, one, one]
    stacked = np.concatenate(rows + [np.zeros((PARTS - 40, P_SIZE), np.float32)], axis=0)
    return np.ascontiguousarray(stacked.T).astype(jnp.bfloat16)


def on_device(
    sources, live_counts, densities, near_list, far_list, far_class, coarse_list, coarse_class, translations,
    check_to_equiv, up_check_to_equiv, partial_check, contrib_ids,
):
    smem = pl.BlockSpec(memory_space=pltpu.SMEM)
    hbm = pl.BlockSpec(memory_space=pl.ANY)
    vmem = pl.BlockSpec(memory_space=pltpu.VMEM)
    dma = pltpu.SemaphoreType.DMA
    f32, bf16, i32 = jnp.float32, jnp.bfloat16, jnp.int32
    sums = pl.pallas_call(
        fmm_kernel,
        out_shape=jax.ShapeDtypeStruct((32, 256), f32),
        in_specs=[smem, smem] + [hbm] * 12,
        out_specs=vmem,
        scratch_shapes=[
            pltpu.VMEM((2, 4, 4, 8, 3, 4, 128), f32),
            pltpu.VMEM((2, 8, 384), f32),
            pltpu.VMEM((3, 8, 384), f32),
            pltpu.VMEM((96, 4, 256), f32),
            pltpu.VMEM((96, P_SIZE), f32),
            pltpu.VMEM((16, 32), i32),
            pltpu.VMEM((16, 32), i32),
            pltpu.VMEM((8, 32), i32),
            pltpu.VMEM((8, 32), i32),
            pltpu.VMEM((16, P_SIZE, P_SIZE), f32),
            pltpu.VMEM((P_SIZE, P_SIZE), f32),
            pltpu.VMEM((P_SIZE, P_SIZE), f32),
            pltpu.VMEM((64, P_SIZE), f32),
            pltpu.VMEM((1, 64), i32),
            pltpu.VMEM((P_SIZE, PARTS), bf16),
            pltpu.VMEM((32, 256, PARTS), bf16),
            pltpu.VMEM((32, PARTS, 256), bf16),
            pltpu.VMEM((PARTS, 1024), f32),
            pltpu.VMEM((PARTS, 1024), f32),
            pltpu.VMEM((8, 1024), f32),
            pltpu.VMEM((8, 1024), f32),
            pltpu.VMEM((P_SIZE, 4864), bf16),
            pltpu.VMEM((P_SIZE, 4864), bf16),
            pltpu.VMEM((512, 384), f32),
            pltpu.VMEM((1024, 384), bf16),
            pltpu.VMEM((1024, 384), bf16),
            pltpu.VMEM((32, P_SIZE, 256), f32),
            pltpu.VMEM((32, 256), f32),
            dma((3,)), dma((3,)), dma((4,)), dma((4,)), dma((7,)), dma((7,)),
            dma((3,)), dma((3,)), dma((4, 3)), dma((4, 3)), dma((16,)), dma((16,)), dma((12,)),
        ],
        compiler_params=pltpu.CompilerParams(
            collective_id=0, has_side_effects=True, vmem_limit_bytes=60 * 1024 * 1024
        ),
    )(
        near_list.T, live_counts, sources, densities.T, far_list.T, far_class.T, coarse_list.T, coarse_class.T,
        translations, check_to_equiv, up_check_to_equiv, partial_check[0].T, contrib_ids,
        jnp.asarray(surface_features()),
    )
    return jnp.where(jnp.arange(256, dtype=jnp.int32)[None, :] < live_counts[:, None], sums, 0.0)


def solution(mesh):
    both = ("gx", "gy")
    return jax.shard_map(
        on_device,
        mesh=mesh,
        in_specs=(
            P(both, None, None), P(both), P(None, both), P(both, None), P(both, None), P(both, None), P(both, None),
            P(both, None), P(), P(), P(), P(both, None, None), P(both, None),
        ),
        out_specs=P(both, None),
        check_vma=False,
    )
```

```python
import jax
import jax.numpy as jnp
import numpy as np
from jax import lax
from jax.experimental import pallas as pl
from jax.experimental.pallas import tpu as pltpu
from jax.sharding import PartitionSpec as P

MESH = pl.DeviceIdType.MESH
ORDER = 8
P_SIZE = 296
SOFT = 0.0625
HALF = 2.5
PARTS = 48
NEAR_SPLIT = (0, 8, 16, 20, 24, 28, 32)


def surface_rows():
    ladder = np.arange(ORDER)
    grid = np.stack(np.meshgrid(ladder, ladder, ladder, indexing="ij")).reshape(3, -1)
    grid = grid[:, ((grid == 0) | (grid == ORDER - 1)).any(axis=0)].astype(np.float32)
    return (-HALF + 2.0 * HALF * grid / (ORDER - 1)).astype(np.float32)


def two(v):
    high = v.astype(jnp.bfloat16).astype(jnp.float32)
    low = (v - high).astype(jnp.bfloat16).astype(jnp.float32)
    return high, low


def three(v):
    high, mid = two(v)
    return high, mid, (v - high - mid).astype(jnp.bfloat16).astype(jnp.float32)


def target_rows(v):
    high, low = two(v)
    seen = high + low
    one = jnp.ones_like(v)
    return (high, high, low, low, one, one, one) + three(seen * seen)


def source_rows(v):
    high, low = two(v)
    seen = high + low
    one = jnp.ones_like(v)
    return (-2.0 * high, -2.0 * low, -2.0 * high, -2.0 * low) + three(seen * seen) + (one, one, one)


def dot_t(a, b):
    return lax.dot_general(a, b, (((1,), (1,)), ((), ())), preferred_element_type=jnp.float32)


def dot_n(a, b):
    return jnp.dot(a, b, preferred_element_type=jnp.float32)


def halves(v):
    high = v.astype(jnp.bfloat16)
    return high, (v - high.astype(jnp.float32)).astype(jnp.bfloat16)


def fmm_kernel(
    near_hbm, live_hbm, src_hbm, dens_hbm, flist_hbm, fclass_hbm, clist_hbm, cclass_hbm, trans_hbm, down_hbm, up_hbm,
    part_hbm, ids_hbm, surf_hbm, out_ref,
    pv_ref, wt, rt, win, dw, flist, fclass, clist, cclass, trans, down, up, part, ids, surf,
    tfeat, tfar, fa, fb, qa, qb, th, tl, gfar, up_high, up_low, pulls, near_rows,
    near_ref, live_ref, p0s, p0r, hs, hr, zs, zr, as_, ar, bs, br, fs, fr, ls,
):
    highest = lax.Precision.HIGHEST
    z = lax.axis_index("gx")
    gy = lax.axis_index("gy")
    x, y, c = gy // 8, (gy // 2) % 4, gy % 2
    chip = z * 16 + x * 4 + y
    d = z * 32 + gy
    partner = (z, gy + 1 - 2 * c)
    a = x + c * (y - x)
    b = y + c * (x - y)

    def chip_dev(q, core):
        return (q // 16, ((q // 4) % 4) * 8 + (q % 4) * 2 + core)

    def ab_dev(a1, b1):
        return (z, (a1 + c * (b1 - a1)) * 8 + (b1 + c * (a1 - b1)) * 2 + c)

    prev_chip = (chip + 127) % 128
    next_chip = (chip + 1) % 128
    adj_chip = (chip + 127 + 2 * c) % 128

    barrier = pltpu.get_barrier_semaphore()
    peers = [partner, chip_dev(prev_chip, 1), chip_dev(next_chip, 0)]
    peers += [((z + k) % 8, gy) for k in (4, 3, 5, 2, 6, 1, 7)]
    peers += [ab_dev((a + k) % 4, b) for k in range(1, 4)]
    peers += [ab_dev(a, (b + k) % 4) for k in range(1, 4)]
    for peer in peers:
        pl.semaphore_signal(barrier, inc=1, device_id=peer, device_id_type=MESH)

    loads = [
        pltpu.make_async_copy(s, t, ls.at[i])
        for i, (s, t) in enumerate(
            (
                (ids_hbm, ids), (part_hbm, part), (up_hbm, up), (src_hbm, win.at[pl.ds(32, 32)]),
                (dens_hbm, dw.at[pl.ds(32, 32)]), (flist_hbm, flist), (fclass_hbm, fclass), (clist_hbm, clist),
                (cclass_hbm, cclass), (surf_hbm, surf), (down_hbm, down), (trans_hbm, trans),
                (near_hbm, near_ref), (live_hbm, live_ref),
            )
        )
    ]
    for load in loads:
        load.start()

    rows = lax.broadcasted_iota(jnp.int32, (16, 64), 0)
    adj_base = 8 * chip - 8 + 16 * c
    wanted = jnp.where(rows < 8, 8 * chip + rows, adj_base + rows - 8)
    wt[...] = jnp.zeros_like(wt)
    for load in loads[0:3]:
        load.wait()
    hot = (wanted == ids[...]).astype(jnp.float32)
    mine = jnp.dot(hot, part[...], precision=highest, preferred_element_type=jnp.float32)
    m_high, m_low = halves(mine)
    u_high, u_low = halves(up[...])
    mine = dot_t(m_high, u_high) + dot_t(m_low, u_high) + dot_t(m_high, u_low)
    wt[0, :, 0:P_SIZE] = mine[0:8]
    wt[1, :, 0:P_SIZE] = mine[8:16]
    pl.semaphore_wait(barrier, len(peers))

    def rcopy(src, dst, ssem, rsem, dev):
        return pltpu.make_async_remote_copy(
            src_ref=src, dst_ref=dst, send_sem=ssem, recv_sem=rsem, device_id=dev, device_id_type=MESH
        )

    sends = []

    def send(src, dst, ssem, rsem, dev):
        cp = rcopy(src, dst, ssem, rsem, dev)
        cp.start()
        sends.append(cp)

    def arrive(dst, rsem):
        rcopy(dst, dst, fs.at[0], rsem, partner).wait_recv()

    send(wt.at[1], rt.at[2 - c], p0s.at[1], p0r.at[2 - c], chip_dev(adj_chip, 0))
    send(wt.at[1], rt.at[2 - c], p0s.at[2], p0r.at[2 - c], chip_dev(adj_chip, 1))
    send(wt.at[0], rt.at[0], p0s.at[0], p0r.at[0], partner)
    loads[3].wait()
    loads[13].wait()
    spot_row = lax.broadcasted_iota(jnp.int32, (4, 256), 0)
    spot_lane = lax.broadcasted_iota(jnp.int32, (4, 256), 1)

    def mask_leaf(t, carry):
        v = win[32 + t]
        win[32 + t] = jnp.where((spot_row == 3) & (spot_lane >= live_ref[t]), 0.0, v)
        return carry

    lax.fori_loop(0, 32, mask_leaf, 0, unroll=4)

    up_d, down_d = (d + 1) % 256, (d + 255) % 256
    up_dev, down_dev = (up_d // 32, up_d % 32), (down_d // 32, down_d % 32)
    own = win.at[pl.ds(32, 32)]
    send(own, win.at[pl.ds(0, 32)], hs.at[0], hr.at[0], up_dev)
    send(own, win.at[pl.ds(64, 32)], hs.at[1], hr.at[1], down_dev)
    send(dens_hbm, dw.at[pl.ds(0, 32)], hs.at[2], hr.at[2], up_dev)
    send(dens_hbm, dw.at[pl.ds(64, 32)], hs.at[3], hr.at[3], down_dev)

    def target_step(t, carry):
        v = jnp.where(spot_row < 3, win[32 + t], 0.0)
        for i, piece in enumerate(target_rows(v)):
            fa[4 * i : 4 * i + 4, 0:256] = piece
        tfeat[t] = jnp.transpose(fa[:, 0:256]).astype(jnp.bfloat16)
        tfar[t] = fa[:, 0:256].astype(jnp.bfloat16)
        return carry

    fa[40:PARTS, :] = jnp.zeros((PARTS - 40, 1024), jnp.float32)
    fb[40:PARTS, :] = jnp.zeros((PARTS - 40, 1024), jnp.float32)
    lax.fori_loop(0, 32, target_step, 0, unroll=4)
    loads[9].wait()
    far_points = surf

    def pull_step(t, carry):
        pulls[t] = lax.rsqrt(dot_n(far_points[...], tfar[t]))
        return carry

    lax.fori_loop(0, 32, pull_step, 0, unroll=8)

    for k in range(3):
        arrive(rt.at[k], p0r.at[k])
    total = wt[0] + rt[0] + rt[1] + rt[2]
    tile = jnp.where(c == 0, total[:, 0:128], total[:, 128:256])
    tail = jnp.where(c == 0, total[0:4, 256:384], total[4:8, 256:384])
    pv_ref[c, b, a, z, 0] = tile[0:4]
    pv_ref[c, b, a, z, 1] = tile[4:8]
    pv_ref[c, b, a, z, 2] = tail
    for k in (4, 3, 5, 2, 6, 1, 7):
        spot = pv_ref.at[c, b, a, z]
        send(spot, spot, zs.at[k - 1], zr.at[k - 1], ((z + k) % 8, gy))

    def prepare(t, feat, charge):
        for n in range(4):
            leaf = near_ref[n, t]
            v = win[jnp.clip(leaf - 32 * d + 32, 0, 95)]
            gap = jnp.where(spot_row == 0, leaf % 32 - t, 0)
            gap = jnp.where(spot_row == 1, (leaf // 32) % 32 - d % 32, gap)
            gap = jnp.where(spot_row == 2, leaf // 1024 - d // 32, gap)
            placed = jnp.where(spot_row < 3, v + 2.0 * gap.astype(jnp.float32), SOFT**0.5)
            for i, piece in enumerate(source_rows(placed)):
                feat[4 * i : 4 * i + 4, 256 * n : 256 * n + 256] = piece
            charge[0:1, 256 * n : 256 * n + 256] = v[3:4]

    def weigh(points, others, weights):
        count = others.shape[1]
        sums = []
        for i in range(0, 256, 64):
            pulled = lax.rsqrt(dot_n(points[i : i + 64], others)) * weights
            acc = pulled[:, 0:128]
            for j in range(128, count, 128):
                acc = acc + pulled[:, j : j + 128]
            sums.append(acc)
        return jnp.sum(jnp.transpose(jnp.concatenate(sums, axis=0)), axis=0, keepdims=True)

    def near_leaf(t, feat, charge):
        near_rows[pl.ds(t, 1), :] = weigh(tfeat[t], feat[...].astype(jnp.bfloat16), charge[0:1, :])

    def near_pair(i, carry):
        t = 2 * i
        prepare(t + 1, fb, qb)
        near_leaf(t, fa, qa)
        prepare(jnp.minimum(t + 2, 31), fa, qa)
        near_leaf(t + 1, fb, qb)
        return carry

    def near_part(k):
        if NEAR_SPLIT[k] < NEAR_SPLIT[k + 1]:
            lax.fori_loop(NEAR_SPLIT[k] // 2, NEAR_SPLIT[k + 1] // 2, near_pair, 0, unroll=2)

    for load in loads[4:9] + loads[10:13]:
        load.wait()

    def split_step(i, carry):
        v = trans[i]
        at = pl.ds(pl.multiple_of(256 * i, 256), 256)
        th[:, at], tl[:, at] = halves(v[:, 0:256])
        return carry

    lax.fori_loop(0, 16, split_step, 0, unroll=2)
    lane = lax.broadcasted_iota(jnp.int32, (P_SIZE, 128), 1)
    blank = jnp.zeros((P_SIZE, 88), jnp.float32)
    for i in range(0, 16, 3):
        packed = jnp.zeros((P_SIZE, 128), jnp.float32)
        for m in range(min(3, 16 - i)):
            piece = jnp.concatenate([trans[i + m, :, 256:P_SIZE], blank], axis=1)
            packed = packed + (pltpu.roll(piece, 40 * m, 1) if m else piece)
        at = 4096 + 128 * (i // 3)
        th[:, at : at + 128], tl[:, at : at + 128] = halves(packed)
    for k in range(2):
        arrive(win.at[pl.ds(64 * k, 32)], hr.at[k])
    prepare(0, fa, qa)
    near_part(0)

    for k in (1, 7, 2, 6, 3, 5, 4):
        arrive(pv_ref.at[c, b, a, (z + 8 - k) % 8], zr.at[k - 1])
    forwards = 0

    def forward(spot):
        nonlocal forwards
        send(spot, spot, fs.at[forwards], fr.at[forwards], partner)
        forwards += 1

    spot = pv_ref.at[c, b, a]
    for k in (2, 1, 3):
        send(spot, spot, as_.at[k - 1], ar.at[k - 1], ab_dev((a + k) % 4, b))
    for k in (1, 3):
        send(spot, spot, bs.at[0, k - 1], br.at[0, k - 1], ab_dev(a, (b + k) % 4))
    forward(spot)

    near_part(1)

    for j in (1, 3, 2):
        spot = pv_ref.at[c, b, (a + 4 - j) % 4]
        arrive(spot, ar.at[j - 1])
        for k in (1, 3):
            send(spot, spot, bs.at[j, k - 1], br.at[j, k - 1], ab_dev(a, (b + k) % 4))
        forward(spot)

    def b_step(j):
        for k in (1, 3):
            spot = pv_ref.at[c, (b + 4 - k) % 4, (a + 4 - j) % 4]
            arrive(spot, br.at[j, k - 1])
            if (j in (0, 3)) == (k == 1):
                send(spot, spot, bs.at[j, 1], br.at[j, 1], ab_dev(a, (b + k) % 4))
            forward(spot)

    near_part(2)
    b_step(0)
    near_part(3)
    b_step(1)
    near_part(4)
    b_step(3)
    near_part(5)
    b_step(2)
    for k in range(2):
        arrive(dw.at[pl.ds(64 * k, 32)], hr.at[2 + k])

    def columns(ref):
        return jnp.transpose(ref[...])

    def choose(cols, count, width):
        lane = lax.broadcasted_iota(jnp.int32, (32, width), 1)
        return jnp.concatenate(
            [(cols[:, k : k + 1] == lane).astype(jnp.float32) for k in range(count)], axis=0
        ).astype(jnp.bfloat16)

    def by_class(ref, count):
        table = ref[...]
        pad = jnp.zeros((count, 96), jnp.int32)
        wide = jnp.concatenate([table, pad], axis=1)
        tiles = []
        for k in range(0, count, 4):
            row = wide[k : k + 1]
            for m in range(1, 4):
                row = row + pltpu.roll(wide[k + m : k + m + 1], 32 * m, 1)
            tiles.append(row)
        row = jnp.concatenate(tiles, axis=1)
        shape = (512, 32 * count)
        line = lax.broadcasted_iota(jnp.int32, shape, 0)
        lane = lax.broadcasted_iota(jnp.int32, shape, 1)
        code = row * 32 + lax.broadcasted_iota(jnp.int32, row.shape, 1) % 32
        return jnp.where(code == line, 1.0, 0.0).astype(jnp.bfloat16)

    far_pick = choose(columns(flist) - 32 * d + 32, 16, 96)
    dens_high, dens_low = halves(dw[...])
    far_high = dot_n(far_pick, dens_high).astype(jnp.bfloat16)
    far_low = dot_n(far_pick, dens_low).astype(jnp.bfloat16)
    far_class = by_class(fclass, 16)
    gfar[...] = jnp.zeros_like(gfar)
    gfar[:, 0:P_SIZE] = dot_n(far_class, far_high) + dot_n(far_class, far_low)

    wanted = clist[...]
    spots = ((wanted // 8) % 16) * 64 + (wanted // 128) * 8 + wanted % 8
    coarse_pick = choose(jnp.transpose(spots), 8, 1024)
    coarse_class = by_class(cclass, 8)
    down_high, down_low = halves(down[...])

    for j in (0, 1, 3, 2):
        spot = pv_ref.at[c, (b + 2) % 4, (a + 4 - j) % 4]
        arrive(spot, br.at[j, 1])
        forward(spot)

    arrive(pv_ref.at[1 - c, a, b], fr.at[0])
    n = 1
    for j in (1, 3, 2):
        arrive(pv_ref.at[1 - c, a, (b + 4 - j) % 4], fr.at[n])
        n += 1
    for j in (0, 1, 3, 2):
        for k in (1, 3):
            arrive(pv_ref.at[1 - c, (a + 4 - k) % 4, (b + 4 - j) % 4], fr.at[n])
            n += 1

    def collect(da, db):
        a1, b1 = (a + da) % 4, (b + db) % 4
        xx, yy = a1 + c * (b1 - a1), b1 + c * (a1 - b1)
        base = (xx * 4 + yy) * 64
        for k in range(4):
            parts = []
            for zz in (2 * k, 2 * k + 1):
                one, two_ = pv_ref[0, yy, xx, zz], pv_ref[1, xx, yy, zz]
                parts.append(
                    jnp.concatenate(
                        [
                            jnp.concatenate([one[0], one[1]], axis=0),
                            jnp.concatenate([two_[0], two_[1]], axis=0),
                            jnp.concatenate([one[2], two_[2]], axis=0),
                        ],
                        axis=1,
                    )
                )
            high, low = halves(jnp.concatenate(parts, axis=0))
            at = pl.ds(pl.multiple_of(base + 16 * k, 16), 16)
            up_high[at, :] = high
            up_low[at, :] = low

    def collect_near(i, carry):
        p, q = i // 3, i % 3
        collect(p + p // 2, q + q // 2)
        return carry

    def collect_far(i, carry):
        collect(2, i)
        return carry

    def collect_side(i, carry):
        collect(i + i // 2, 2)
        return carry

    lax.fori_loop(0, 9, collect_near, 0, unroll=3)
    for j in (0, 1, 3, 2):
        arrive(pv_ref.at[1 - c, (a + 2) % 4, (b + 4 - j) % 4], fr.at[n])
        n += 1
    lax.fori_loop(0, 4, collect_far, 0, unroll=2)
    lax.fori_loop(0, 3, collect_side, 0, unroll=3)
    coarse_high = dot_n(coarse_pick, up_high[...]).astype(jnp.bfloat16)
    coarse_low = dot_n(coarse_pick, up_low[...]).astype(jnp.bfloat16)
    gathered = gfar[...] + dot_n(coarse_class, coarse_high) + dot_n(coarse_class, coarse_low)
    ends = []
    for i in range(0, 16, 3):
        packed = gathered[32 * i : 32 * i + 32, 256:384]
        for m in range(1, min(3, 16 - i)):
            packed = packed + pltpu.roll(gathered[32 * (i + m) : 32 * (i + m) + 32, 256:384], 40 * m, 1)
        ends.append(packed)
    spread = jnp.concatenate([gathered[32 * i : 32 * i + 32, 0:256] for i in range(16)] + ends, axis=1)
    g_high, g_low = halves(spread)
    wide_sum = dot_t(th[...], jnp.concatenate([g_high, g_low], axis=0))
    check = wide_sum[:, 0:32] + wide_sum[:, 32:64] + dot_t(tl[...], g_high)
    c_high, c_low = halves(check)
    equiv = dot_n(down_high, c_high) + dot_n(down_high, c_low) + dot_n(down_low, c_high)
    for t in range(32):
        far = jnp.sum(equiv[:, t : t + 1] * pulls[t], axis=0, keepdims=True)
        out_ref[t : t + 1, :] = near_rows[t : t + 1, :] + far
    for cp in sends:
        cp.wait_send()


def surface_features():
    points = np.concatenate([surface_rows(), np.full((1, P_SIZE), SOFT**0.5, np.float32)], axis=0)

    def short(v):
        return v.astype(jnp.bfloat16).astype(np.float32)

    high = short(points)
    low = short(points - high)
    seen = high + low
    square = seen * seen
    s1 = short(square)
    s2 = short(square - s1)
    s3 = short(square - s1 - s2)
    one = np.ones_like(points)
    rows = [-2 * high, -2 * low, -2 * high, -2 * low, s1, s2, s3, one, one, one]
    stacked = np.concatenate(rows + [np.zeros((PARTS - 40, P_SIZE), np.float32)], axis=0)
    return np.ascontiguousarray(stacked.T).astype(jnp.bfloat16)


def on_device(
    sources, live_counts, densities, near_list, far_list, far_class, coarse_list, coarse_class, translations,
    check_to_equiv, up_check_to_equiv, partial_check, contrib_ids,
):
    hbm = pl.BlockSpec(memory_space=pl.ANY)
    vmem = pl.BlockSpec(memory_space=pltpu.VMEM)
    dma = pltpu.SemaphoreType.DMA
    f32, bf16, i32 = jnp.float32, jnp.bfloat16, jnp.int32
    sums = pl.pallas_call(
        fmm_kernel,
        out_shape=jax.ShapeDtypeStruct((32, 256), f32),
        in_specs=[hbm] * 14,
        out_specs=vmem,
        scratch_shapes=[
            pltpu.VMEM((2, 4, 4, 8, 3, 4, 128), f32),
            pltpu.VMEM((2, 8, 384), f32),
            pltpu.VMEM((3, 8, 384), f32),
            pltpu.VMEM((96, 4, 256), f32),
            pltpu.VMEM((96, P_SIZE), f32),
            pltpu.VMEM((16, 32), i32),
            pltpu.VMEM((16, 32), i32),
            pltpu.VMEM((8, 32), i32),
            pltpu.VMEM((8, 32), i32),
            pltpu.VMEM((16, P_SIZE, P_SIZE), f32),
            pltpu.VMEM((P_SIZE, P_SIZE), f32),
            pltpu.VMEM((P_SIZE, P_SIZE), f32),
            pltpu.VMEM((64, P_SIZE), f32),
            pltpu.VMEM((1, 64), i32),
            pltpu.VMEM((P_SIZE, PARTS), bf16),
            pltpu.VMEM((32, 256, PARTS), bf16),
            pltpu.VMEM((32, PARTS, 256), bf16),
            pltpu.VMEM((PARTS, 1024), f32),
            pltpu.VMEM((PARTS, 1024), f32),
            pltpu.VMEM((8, 1024), f32),
            pltpu.VMEM((8, 1024), f32),
            pltpu.VMEM((P_SIZE, 4864), bf16),
            pltpu.VMEM((P_SIZE, 4864), bf16),
            pltpu.VMEM((512, 384), f32),
            pltpu.VMEM((1024, 384), bf16),
            pltpu.VMEM((1024, 384), bf16),
            pltpu.VMEM((32, P_SIZE, 256), f32),
            pltpu.VMEM((32, 256), f32),
            pltpu.SMEM((4, 32), i32),
            pltpu.SMEM((32,), i32),
            dma((3,)), dma((3,)), dma((4,)), dma((4,)), dma((7,)), dma((7,)),
            dma((3,)), dma((3,)), dma((4, 3)), dma((4, 3)), dma((16,)), dma((16,)), dma((14,)),
        ],
        compiler_params=pltpu.CompilerParams(
            collective_id=0, has_side_effects=True, vmem_limit_bytes=60 * 1024 * 1024
        ),
    )(
        near_list.T, live_counts, sources, densities.T, far_list.T, far_class.T, coarse_list.T, coarse_class.T,
        translations, check_to_equiv, up_check_to_equiv, partial_check[0].T, contrib_ids,
        jnp.asarray(surface_features()),
    )
    return jnp.where(jnp.arange(256, dtype=jnp.int32)[None, :] < live_counts[:, None], sums, 0.0)


def solution(mesh):
    both = ("gx", "gy")
    return jax.shard_map(
        on_device,
        mesh=mesh,
        in_specs=(
            P(both, None, None), P(both), P(None, both), P(both, None), P(both, None), P(both, None), P(both, None),
            P(both, None), P(), P(), P(), P(both, None, None), P(both, None),
        ),
        out_specs=P(both, None),
        check_vma=False,
    )
```

```python
import jax
import jax.numpy as jnp
import numpy as np
from jax import lax
from jax.experimental import pallas as pl
from jax.experimental.pallas import tpu as pltpu
from jax.sharding import PartitionSpec as P

MESH = pl.DeviceIdType.MESH
ORDER = 8
P_SIZE = 296
SOFT = 0.0625
HALF = 2.5
PARTS = 48
NEAR_SPLIT = (0, 8, 16, 20, 24, 28, 32)


def surface_rows():
    ladder = np.arange(ORDER)
    grid = np.stack(np.meshgrid(ladder, ladder, ladder, indexing="ij")).reshape(3, -1)
    grid = grid[:, ((grid == 0) | (grid == ORDER - 1)).any(axis=0)].astype(np.float32)
    return (-HALF + 2.0 * HALF * grid / (ORDER - 1)).astype(np.float32)


def two(v):
    high = v.astype(jnp.bfloat16).astype(jnp.float32)
    low = (v - high).astype(jnp.bfloat16).astype(jnp.float32)
    return high, low


def three(v):
    high, mid = two(v)
    return high, mid, (v - high - mid).astype(jnp.bfloat16).astype(jnp.float32)


def target_rows(v):
    high, low = two(v)
    seen = high + low
    one = jnp.ones_like(v)
    return (high, high, low, low, one, one, one) + three(seen * seen)


def source_rows(v):
    high, low = two(v)
    seen = high + low
    one = jnp.ones_like(v)
    return (-2.0 * high, -2.0 * low, -2.0 * high, -2.0 * low) + three(seen * seen) + (one, one, one)


def dot_t(a, b):
    return lax.dot_general(a, b, (((1,), (1,)), ((), ())), preferred_element_type=jnp.float32)


def dot_n(a, b):
    return jnp.dot(a, b, preferred_element_type=jnp.float32)


def halves(v):
    high = v.astype(jnp.bfloat16)
    return high, (v - high.astype(jnp.float32)).astype(jnp.bfloat16)


def fmm_kernel(
    near_hbm, live_hbm, src_hbm, dens_hbm, flist_hbm, fclass_hbm, clist_hbm, cclass_hbm, trans_hbm, down_hbm, up_hbm,
    part_hbm, ids_hbm, surf_hbm, out_ref,
    pv_ref, wt, rt, win, dw, flist, fclass, clist, cclass, trans, down, up, part, ids, surf,
    tfeat, tfar, fa, fb, qa, qb, th, tl, gfar, up_both, pulls, near_rows,
    near_ref, live_ref, p0s, p0r, hs, hr, zs, zr, as_, ar, bs, br, fs, fr, ls,
):
    highest = lax.Precision.HIGHEST
    z = lax.axis_index("gx")
    gy = lax.axis_index("gy")
    x, y, c = gy // 8, (gy // 2) % 4, gy % 2
    chip = z * 16 + x * 4 + y
    d = z * 32 + gy
    partner = (z, gy + 1 - 2 * c)
    a = x + c * (y - x)
    b = y + c * (x - y)

    def chip_dev(q, core):
        return (q // 16, ((q // 4) % 4) * 8 + (q % 4) * 2 + core)

    def ab_dev(a1, b1):
        return (z, (a1 + c * (b1 - a1)) * 8 + (b1 + c * (a1 - b1)) * 2 + c)

    prev_chip = (chip + 127) % 128
    next_chip = (chip + 1) % 128
    adj_chip = (chip + 127 + 2 * c) % 128

    barrier = pltpu.get_barrier_semaphore()
    peers = [partner, chip_dev(prev_chip, 1), chip_dev(next_chip, 0)]
    peers += [((z + k) % 8, gy) for k in (4, 3, 5, 2, 6, 1, 7)]
    peers += [ab_dev((a + k) % 4, b) for k in range(1, 4)]
    peers += [ab_dev(a, (b + k) % 4) for k in range(1, 4)]
    for peer in peers:
        pl.semaphore_signal(barrier, inc=1, device_id=peer, device_id_type=MESH)

    loads = [
        pltpu.make_async_copy(s, t, ls.at[i])
        for i, (s, t) in enumerate(
            (
                (ids_hbm, ids), (part_hbm, part), (up_hbm, up), (src_hbm, win.at[pl.ds(32, 32)]),
                (dens_hbm, dw.at[pl.ds(32, 32)]), (flist_hbm, flist), (fclass_hbm, fclass), (clist_hbm, clist),
                (cclass_hbm, cclass), (surf_hbm, surf), (down_hbm, down), (trans_hbm, trans),
                (near_hbm, near_ref), (live_hbm, live_ref),
            )
        )
    ]
    for load in loads:
        load.start()

    rows = lax.broadcasted_iota(jnp.int32, (16, 64), 0)
    adj_base = 8 * chip - 8 + 16 * c
    wanted = jnp.where(rows < 8, 8 * chip + rows, adj_base + rows - 8)
    wt[...] = jnp.zeros_like(wt)
    for load in loads[0:3]:
        load.wait()
    hot = (wanted == ids[...]).astype(jnp.float32)
    mine = jnp.dot(hot, part[...], precision=highest, preferred_element_type=jnp.float32)
    m_high, m_low = halves(mine)
    u_high, u_low = halves(up[...])
    mine = dot_t(m_high, u_high) + dot_t(m_low, u_high) + dot_t(m_high, u_low)
    wt[0, :, 0:P_SIZE] = mine[0:8]
    wt[1, :, 0:P_SIZE] = mine[8:16]
    pl.semaphore_wait(barrier, len(peers))

    def rcopy(src, dst, ssem, rsem, dev):
        return pltpu.make_async_remote_copy(
            src_ref=src, dst_ref=dst, send_sem=ssem, recv_sem=rsem, device_id=dev, device_id_type=MESH
        )

    sends = []

    def send(src, dst, ssem, rsem, dev):
        cp = rcopy(src, dst, ssem, rsem, dev)
        cp.start()
        sends.append(cp)

    def arrive(dst, rsem):
        rcopy(dst, dst, fs.at[0], rsem, partner).wait_recv()

    send(wt.at[1], rt.at[2 - c], p0s.at[1], p0r.at[2 - c], chip_dev(adj_chip, 0))
    send(wt.at[1], rt.at[2 - c], p0s.at[2], p0r.at[2 - c], chip_dev(adj_chip, 1))
    send(wt.at[0], rt.at[0], p0s.at[0], p0r.at[0], partner)
    loads[3].wait()
    loads[13].wait()
    spot_row = lax.broadcasted_iota(jnp.int32, (4, 256), 0)
    spot_lane = lax.broadcasted_iota(jnp.int32, (4, 256), 1)

    def mask_leaf(t, carry):
        v = win[32 + t]
        win[32 + t] = jnp.where((spot_row == 3) & (spot_lane >= live_ref[t]), 0.0, v)
        return carry

    lax.fori_loop(0, 32, mask_leaf, 0, unroll=4)

    up_d, down_d = (d + 1) % 256, (d + 255) % 256
    up_dev, down_dev = (up_d // 32, up_d % 32), (down_d // 32, down_d % 32)
    own = win.at[pl.ds(32, 32)]
    send(own, win.at[pl.ds(0, 32)], hs.at[0], hr.at[0], up_dev)
    send(own, win.at[pl.ds(64, 32)], hs.at[1], hr.at[1], down_dev)
    send(dens_hbm, dw.at[pl.ds(0, 32)], hs.at[2], hr.at[2], up_dev)
    send(dens_hbm, dw.at[pl.ds(64, 32)], hs.at[3], hr.at[3], down_dev)

    def target_step(t, carry):
        v = jnp.where(spot_row < 3, win[32 + t], 0.0)
        for i, piece in enumerate(target_rows(v)):
            fa[4 * i : 4 * i + 4, 0:256] = piece
        tfeat[t] = jnp.transpose(fa[:, 0:256]).astype(jnp.bfloat16)
        tfar[t] = fa[:, 0:256].astype(jnp.bfloat16)
        return carry

    fa[40:PARTS, :] = jnp.zeros((PARTS - 40, 1024), jnp.float32)
    fb[40:PARTS, :] = jnp.zeros((PARTS - 40, 1024), jnp.float32)
    lax.fori_loop(0, 32, target_step, 0, unroll=4)
    loads[9].wait()
    far_points = surf

    def pull_step(t, carry):
        pulls[t] = lax.rsqrt(dot_n(far_points[...], tfar[t]))
        return carry

    lax.fori_loop(0, 32, pull_step, 0, unroll=8)

    for k in range(3):
        arrive(rt.at[k], p0r.at[k])
    total = wt[0] + rt[0] + rt[1] + rt[2]
    tile = jnp.where(c == 0, total[:, 0:128], total[:, 128:256])
    tail = jnp.where(c == 0, total[0:4, 256:384], total[4:8, 256:384])
    pv_ref[c, b, a, z, 0] = tile[0:4]
    pv_ref[c, b, a, z, 1] = tile[4:8]
    pv_ref[c, b, a, z, 2] = tail
    for k in (4, 3, 5, 2, 6, 1, 7):
        spot = pv_ref.at[c, b, a, z]
        send(spot, spot, zs.at[k - 1], zr.at[k - 1], ((z + k) % 8, gy))

    def prepare(t, feat, charge):
        for n in range(4):
            leaf = near_ref[n, t]
            v = win[jnp.clip(leaf - 32 * d + 32, 0, 95)]
            gap = jnp.where(spot_row == 0, leaf % 32 - t, 0)
            gap = jnp.where(spot_row == 1, (leaf // 32) % 32 - d % 32, gap)
            gap = jnp.where(spot_row == 2, leaf // 1024 - d // 32, gap)
            placed = jnp.where(spot_row < 3, v + 2.0 * gap.astype(jnp.float32), SOFT**0.5)
            for i, piece in enumerate(source_rows(placed)):
                feat[4 * i : 4 * i + 4, 256 * n : 256 * n + 256] = piece
            charge[0:1, 256 * n : 256 * n + 256] = v[3:4]

    def weigh(points, others, weights):
        count = others.shape[1]
        sums = []
        for i in range(0, 256, 64):
            pulled = lax.rsqrt(dot_n(points[i : i + 64], others)) * weights
            acc = pulled[:, 0:128]
            for j in range(128, count, 128):
                acc = acc + pulled[:, j : j + 128]
            sums.append(acc)
        return jnp.sum(jnp.transpose(jnp.concatenate(sums, axis=0)), axis=0, keepdims=True)

    def near_leaf(t, feat, charge):
        near_rows[pl.ds(t, 1), :] = weigh(tfeat[t], feat[...].astype(jnp.bfloat16), charge[0:1, :])

    def near_pair(i, carry):
        t = 2 * i
        prepare(t + 1, fb, qb)
        near_leaf(t, fa, qa)
        prepare(jnp.minimum(t + 2, 31), fa, qa)
        near_leaf(t + 1, fb, qb)
        return carry

    def near_part(k):
        if NEAR_SPLIT[k] < NEAR_SPLIT[k + 1]:
            lax.fori_loop(NEAR_SPLIT[k] // 2, NEAR_SPLIT[k + 1] // 2, near_pair, 0, unroll=2)

    for load in loads[4:9] + loads[10:13]:
        load.wait()

    def split_step(i, carry):
        v = trans[i]
        at = pl.ds(pl.multiple_of(256 * i, 256), 256)
        th[:, at], tl[:, at] = halves(v[:, 0:256])
        return carry

    lax.fori_loop(0, 16, split_step, 0, unroll=2)
    lane = lax.broadcasted_iota(jnp.int32, (P_SIZE, 128), 1)
    blank = jnp.zeros((P_SIZE, 88), jnp.float32)
    for i in range(0, 16, 3):
        packed = jnp.zeros((P_SIZE, 128), jnp.float32)
        for m in range(min(3, 16 - i)):
            piece = jnp.concatenate([trans[i + m, :, 256:P_SIZE], blank], axis=1)
            packed = packed + (pltpu.roll(piece, 40 * m, 1) if m else piece)
        at = 4096 + 128 * (i // 3)
        th[:, at : at + 128], tl[:, at : at + 128] = halves(packed)
    for k in range(2):
        arrive(win.at[pl.ds(64 * k, 32)], hr.at[k])
    prepare(0, fa, qa)
    near_part(0)

    for k in (1, 7, 2, 6, 3, 5, 4):
        arrive(pv_ref.at[c, b, a, (z + 8 - k) % 8], zr.at[k - 1])
    forwards = 0

    def forward(spot):
        nonlocal forwards
        send(spot, spot, fs.at[forwards], fr.at[forwards], partner)
        forwards += 1

    spot = pv_ref.at[c, b, a]
    for k in (2, 1, 3):
        send(spot, spot, as_.at[k - 1], ar.at[k - 1], ab_dev((a + k) % 4, b))
    for k in (1, 3):
        send(spot, spot, bs.at[0, k - 1], br.at[0, k - 1], ab_dev(a, (b + k) % 4))
    forward(spot)

    near_part(1)

    for j in (1, 3, 2):
        spot = pv_ref.at[c, b, (a + 4 - j) % 4]
        arrive(spot, ar.at[j - 1])
        for k in (1, 3):
            send(spot, spot, bs.at[j, k - 1], br.at[j, k - 1], ab_dev(a, (b + k) % 4))
        forward(spot)

    def b_step(j):
        for k in (1, 3):
            spot = pv_ref.at[c, (b + 4 - k) % 4, (a + 4 - j) % 4]
            arrive(spot, br.at[j, k - 1])
            if (j in (0, 3)) == (k == 1):
                send(spot, spot, bs.at[j, 1], br.at[j, 1], ab_dev(a, (b + k) % 4))
            forward(spot)

    near_part(2)
    near_part(3)
    b_step(0)
    near_part(4)
    b_step(1)
    b_step(3)
    b_step(2)
    near_part(5)
    for k in range(2):
        arrive(dw.at[pl.ds(64 * k, 32)], hr.at[2 + k])

    def columns(ref):
        return jnp.transpose(ref[...])

    def choose(cols, count, width):
        lane = lax.broadcasted_iota(jnp.int32, (32, width), 1)
        return jnp.concatenate(
            [(cols[:, k : k + 1] == lane).astype(jnp.float32) for k in range(count)], axis=0
        ).astype(jnp.bfloat16)

    def by_class(ref, count):
        table = ref[...]
        pad = jnp.zeros((count, 96), jnp.int32)
        wide = jnp.concatenate([table, pad], axis=1)
        tiles = []
        for k in range(0, count, 4):
            row = wide[k : k + 1]
            for m in range(1, 4):
                row = row + pltpu.roll(wide[k + m : k + m + 1], 32 * m, 1)
            tiles.append(row)
        row = jnp.concatenate(tiles, axis=1)
        shape = (512, 32 * count)
        line = lax.broadcasted_iota(jnp.int32, shape, 0)
        lane = lax.broadcasted_iota(jnp.int32, shape, 1)
        code = row * 32 + lax.broadcasted_iota(jnp.int32, row.shape, 1) % 32
        return jnp.where(code == line, 1.0, 0.0).astype(jnp.bfloat16)

    far_pick = choose(columns(flist) - 32 * d + 32, 16, 96)
    dens_high, dens_low = halves(dw[...])
    far_high = dot_n(far_pick, dens_high).astype(jnp.bfloat16)
    far_low = dot_n(far_pick, dens_low).astype(jnp.bfloat16)
    far_class = by_class(fclass, 16)
    gfar[...] = jnp.zeros_like(gfar)
    gfar[:, 0:P_SIZE] = dot_n(far_class, far_high) + dot_n(far_class, far_low)

    wanted = clist[...]
    spots = ((wanted // 8) % 16) * 64 + (wanted // 128) * 8 + wanted % 8
    coarse_pick = choose(jnp.transpose(spots), 8, 1024)
    coarse_class = by_class(cclass, 8)
    down_high, down_low = halves(down[...])

    for j in (0, 1, 3, 2):
        spot = pv_ref.at[c, (b + 2) % 4, (a + 4 - j) % 4]
        arrive(spot, br.at[j, 1])
        forward(spot)

    arrive(pv_ref.at[1 - c, a, b], fr.at[0])
    n = 1
    for j in (1, 3, 2):
        arrive(pv_ref.at[1 - c, a, (b + 4 - j) % 4], fr.at[n])
        n += 1
    for j in (0, 1, 3, 2):
        for k in (1, 3):
            arrive(pv_ref.at[1 - c, (a + 4 - k) % 4, (b + 4 - j) % 4], fr.at[n])
            n += 1

    def collect(da, db):
        a1, b1 = (a + da) % 4, (b + db) % 4
        xx, yy = a1 + c * (b1 - a1), b1 + c * (a1 - b1)
        base = (xx * 4 + yy) * 64
        for k in range(4):
            parts = []
            for zz in (2 * k, 2 * k + 1):
                one, two_ = pv_ref[0, yy, xx, zz], pv_ref[1, xx, yy, zz]
                parts.append(
                    jnp.concatenate(
                        [
                            jnp.concatenate([one[0], one[1]], axis=0),
                            jnp.concatenate([two_[0], two_[1]], axis=0),
                            jnp.concatenate([one[2], two_[2]], axis=0),
                        ],
                        axis=1,
                    )
                )
            high, low = halves(jnp.concatenate(parts, axis=0))
            at = pl.ds(pl.multiple_of(base + 16 * k, 16), 16)
            up_both[at, 0:384] = high
            up_both[at, 384:768] = low

    def collect_near(i, carry):
        p, q = i // 3, i % 3
        collect(p + p // 2, q + q // 2)
        return carry

    def collect_far(i, carry):
        collect(2, i)
        return carry

    def collect_side(i, carry):
        collect(i + i // 2, 2)
        return carry

    lax.fori_loop(0, 9, collect_near, 0, unroll=3)
    for j in (0, 1, 3, 2):
        arrive(pv_ref.at[1 - c, (a + 2) % 4, (b + 4 - j) % 4], fr.at[n])
        n += 1
    lax.fori_loop(0, 4, collect_far, 0, unroll=2)
    lax.fori_loop(0, 3, collect_side, 0, unroll=3)
    coarse = dot_n(coarse_class, dot_n(coarse_pick, up_both[...]).astype(jnp.bfloat16))
    gathered = gfar[...] + coarse[:, 0:384] + coarse[:, 384:768]
    ends = []
    for i in range(0, 16, 3):
        packed = gathered[32 * i : 32 * i + 32, 256:384]
        for m in range(1, min(3, 16 - i)):
            packed = packed + pltpu.roll(gathered[32 * (i + m) : 32 * (i + m) + 32, 256:384], 40 * m, 1)
        ends.append(packed)
    spread = jnp.concatenate([gathered[32 * i : 32 * i + 32, 0:256] for i in range(16)] + ends, axis=1)
    g_high, g_low = halves(spread)
    wide_sum = dot_t(th[...], jnp.concatenate([g_high, g_low], axis=0))
    check = wide_sum[:, 0:32] + wide_sum[:, 32:64] + dot_t(tl[...], g_high)
    c_high, c_low = halves(check)
    equiv = dot_n(down_high, c_high) + dot_n(down_high, c_low) + dot_n(down_low, c_high)
    for t in range(32):
        acc = jnp.zeros((8, 256), jnp.float32)
        for lo in range(0, P_SIZE, 64):
            hi = min(lo + 64, P_SIZE)
            part_sum = equiv[lo:hi, t : t + 1] * pulls[t, lo:hi, :]
            acc = acc + jnp.sum(part_sum.reshape((hi - lo) // 8, 8, 256), axis=0)
        far = jnp.sum(acc, axis=0, keepdims=True)
        out_ref[t : t + 1, :] = near_rows[t : t + 1, :] + far
    for cp in sends:
        cp.wait_send()


def surface_features():
    points = np.concatenate([surface_rows(), np.full((1, P_SIZE), SOFT**0.5, np.float32)], axis=0)

    def short(v):
        return v.astype(jnp.bfloat16).astype(np.float32)

    high = short(points)
    low = short(points - high)
    seen = high + low
    square = seen * seen
    s1 = short(square)
    s2 = short(square - s1)
    s3 = short(square - s1 - s2)
    one = np.ones_like(points)
    rows = [-2 * high, -2 * low, -2 * high, -2 * low, s1, s2, s3, one, one, one]
    stacked = np.concatenate(rows + [np.zeros((PARTS - 40, P_SIZE), np.float32)], axis=0)
    return np.ascontiguousarray(stacked.T).astype(jnp.bfloat16)


def on_device(
    sources, live_counts, densities, near_list, far_list, far_class, coarse_list, coarse_class, translations,
    check_to_equiv, up_check_to_equiv, partial_check, contrib_ids,
):
    hbm = pl.BlockSpec(memory_space=pl.ANY)
    vmem = pl.BlockSpec(memory_space=pltpu.VMEM)
    dma = pltpu.SemaphoreType.DMA
    f32, bf16, i32 = jnp.float32, jnp.bfloat16, jnp.int32
    sums = pl.pallas_call(
        fmm_kernel,
        out_shape=jax.ShapeDtypeStruct((32, 256), f32),
        in_specs=[hbm] * 14,
        out_specs=vmem,
        scratch_shapes=[
            pltpu.VMEM((2, 4, 4, 8, 3, 4, 128), f32),
            pltpu.VMEM((2, 8, 384), f32),
            pltpu.VMEM((3, 8, 384), f32),
            pltpu.VMEM((96, 4, 256), f32),
            pltpu.VMEM((96, P_SIZE), f32),
            pltpu.VMEM((16, 32), i32),
            pltpu.VMEM((16, 32), i32),
            pltpu.VMEM((8, 32), i32),
            pltpu.VMEM((8, 32), i32),
            pltpu.VMEM((16, P_SIZE, P_SIZE), f32),
            pltpu.VMEM((P_SIZE, P_SIZE), f32),
            pltpu.VMEM((P_SIZE, P_SIZE), f32),
            pltpu.VMEM((64, P_SIZE), f32),
            pltpu.VMEM((1, 64), i32),
            pltpu.VMEM((P_SIZE, PARTS), bf16),
            pltpu.VMEM((32, 256, PARTS), bf16),
            pltpu.VMEM((32, PARTS, 256), bf16),
            pltpu.VMEM((PARTS, 1024), f32),
            pltpu.VMEM((PARTS, 1024), f32),
            pltpu.VMEM((8, 1024), f32),
            pltpu.VMEM((8, 1024), f32),
            pltpu.VMEM((P_SIZE, 4864), bf16),
            pltpu.VMEM((P_SIZE, 4864), bf16),
            pltpu.VMEM((512, 384), f32),
            pltpu.VMEM((1024, 768), bf16),
            pltpu.VMEM((32, P_SIZE, 256), f32),
            pltpu.VMEM((32, 256), f32),
            pltpu.SMEM((4, 32), i32),
            pltpu.SMEM((32,), i32),
            dma((3,)), dma((3,)), dma((4,)), dma((4,)), dma((7,)), dma((7,)),
            dma((3,)), dma((3,)), dma((4, 3)), dma((4, 3)), dma((16,)), dma((16,)), dma((14,)),
        ],
        compiler_params=pltpu.CompilerParams(
            collective_id=0, has_side_effects=True, vmem_limit_bytes=57 * 1024 * 1024
        ),
    )(
        near_list.T, live_counts, sources, densities.T, far_list.T, far_class.T, coarse_list.T, coarse_class.T,
        translations, check_to_equiv, up_check_to_equiv, partial_check[0].T, contrib_ids,
        jnp.asarray(surface_features()),
    )
    return jnp.where(jnp.arange(256, dtype=jnp.int32)[None, :] < live_counts[:, None], sums, 0.0)


def solution(mesh):
    both = ("gx", "gy")
    return jax.shard_map(
        on_device,
        mesh=mesh,
        in_specs=(
            P(both, None, None), P(both), P(None, both), P(both, None), P(both, None), P(both, None), P(both, None),
            P(both, None), P(), P(), P(), P(both, None, None), P(both, None),
        ),
        out_specs=P(both, None),
        check_vma=False,
    )
```

```python
import jax
import jax.numpy as jnp
import numpy as np
from jax import lax
from jax.experimental import pallas as pl
from jax.experimental.pallas import tpu as pltpu
from jax.sharding import PartitionSpec as P

MESH = pl.DeviceIdType.MESH
ORDER = 8
P_SIZE = 296
SOFT = 0.0625
HALF = 2.5
PARTS = 48
NEAR_SPLIT = (0, 8, 16, 20, 24, 28, 32)


def surface_rows():
    ladder = np.arange(ORDER)
    grid = np.stack(np.meshgrid(ladder, ladder, ladder, indexing="ij")).reshape(3, -1)
    grid = grid[:, ((grid == 0) | (grid == ORDER - 1)).any(axis=0)].astype(np.float32)
    return (-HALF + 2.0 * HALF * grid / (ORDER - 1)).astype(np.float32)


def two(v):
    high = v.astype(jnp.bfloat16).astype(jnp.float32)
    low = (v - high).astype(jnp.bfloat16).astype(jnp.float32)
    return high, low


def three(v):
    high, mid = two(v)
    return high, mid, (v - high - mid).astype(jnp.bfloat16).astype(jnp.float32)


def target_rows(v):
    high, low = two(v)
    seen = high + low
    one = jnp.ones_like(v)
    return (high, high, low, low, one, one, one) + three(seen * seen)


def source_rows(v):
    high, low = two(v)
    seen = high + low
    one = jnp.ones_like(v)
    return (-2.0 * high, -2.0 * low, -2.0 * high, -2.0 * low) + three(seen * seen) + (one, one, one)


def dot_t(a, b):
    return lax.dot_general(a, b, (((1,), (1,)), ((), ())), preferred_element_type=jnp.float32)


def dot_n(a, b):
    return jnp.dot(a, b, preferred_element_type=jnp.float32)


def halves(v):
    high = v.astype(jnp.bfloat16)
    return high, (v - high.astype(jnp.float32)).astype(jnp.bfloat16)


def fmm_kernel(
    near_hbm, live_hbm, src_hbm, dens_hbm, flist_hbm, fclass_hbm, clist_hbm, cclass_hbm, trans_hbm, down_hbm, up_hbm,
    part_hbm, ids_hbm, surf_hbm, out_ref,
    pv_ref, wt, rt, win, dw, flist, fclass, clist, cclass, trans, down, up, part, ids, surf,
    tfeat, tfar, fa, fb, qa, qb, th, tl, gfar, up_high, up_low, pulls, near_rows,
    near_ref, live_ref, p0s, p0r, hs, hr, zs, zr, as_, ar, bs, br, fs, fr, ls,
):
    highest = lax.Precision.HIGHEST
    z = lax.axis_index("gx")
    gy = lax.axis_index("gy")
    x, y, c = gy // 8, (gy // 2) % 4, gy % 2
    chip = z * 16 + x * 4 + y
    d = z * 32 + gy
    partner = (z, gy + 1 - 2 * c)
    a = x + c * (y - x)
    b = y + c * (x - y)

    def chip_dev(q, core):
        return (q // 16, ((q // 4) % 4) * 8 + (q % 4) * 2 + core)

    def ab_dev(a1, b1):
        return (z, (a1 + c * (b1 - a1)) * 8 + (b1 + c * (a1 - b1)) * 2 + c)

    prev_chip = (chip + 127) % 128
    next_chip = (chip + 1) % 128
    adj_chip = (chip + 127 + 2 * c) % 128

    barrier = pltpu.get_barrier_semaphore()
    peers = [partner, chip_dev(prev_chip, 1), chip_dev(next_chip, 0)]
    peers += [((z + k) % 8, gy) for k in (4, 3, 5, 2, 6, 1, 7)]
    peers += [ab_dev((a + k) % 4, b) for k in range(1, 4)]
    peers += [ab_dev(a, (b + k) % 4) for k in range(1, 4)]
    for peer in peers:
        pl.semaphore_signal(barrier, inc=1, device_id=peer, device_id_type=MESH)

    loads = [
        pltpu.make_async_copy(s, t, ls.at[i])
        for i, (s, t) in enumerate(
            (
                (ids_hbm, ids), (part_hbm, part), (up_hbm, up), (src_hbm, win.at[pl.ds(32, 32)]),
                (dens_hbm, dw.at[pl.ds(32, 32)]), (flist_hbm, flist), (fclass_hbm, fclass), (clist_hbm, clist),
                (cclass_hbm, cclass), (surf_hbm, surf), (down_hbm, down), (trans_hbm, trans),
                (near_hbm, near_ref), (live_hbm, live_ref),
            )
        )
    ]
    for load in loads:
        load.start()

    rows = lax.broadcasted_iota(jnp.int32, (16, 64), 0)
    adj_base = 8 * chip - 8 + 16 * c
    wanted = jnp.where(rows < 8, 8 * chip + rows, adj_base + rows - 8)
    wt[...] = jnp.zeros_like(wt)
    for load in loads[0:3]:
        load.wait()
    hot = (wanted == ids[...]).astype(jnp.float32)
    mine = jnp.dot(hot, part[...], precision=highest, preferred_element_type=jnp.float32)
    m_high, m_low = halves(mine)
    u_high, u_low = halves(up[...])
    mine = dot_t(m_high, u_high) + dot_t(m_low, u_high) + dot_t(m_high, u_low)
    wt[0, :, 0:P_SIZE] = mine[0:8]
    wt[1, :, 0:P_SIZE] = mine[8:16]
    pl.semaphore_wait(barrier, len(peers))

    def rcopy(src, dst, ssem, rsem, dev):
        return pltpu.make_async_remote_copy(
            src_ref=src, dst_ref=dst, send_sem=ssem, recv_sem=rsem, device_id=dev, device_id_type=MESH
        )

    sends = []

    def send(src, dst, ssem, rsem, dev):
        cp = rcopy(src, dst, ssem, rsem, dev)
        cp.start()
        sends.append(cp)

    def arrive(dst, rsem):
        rcopy(dst, dst, fs.at[0], rsem, partner).wait_recv()

    send(wt.at[1], rt.at[2 - c], p0s.at[1], p0r.at[2 - c], chip_dev(adj_chip, 0))
    send(wt.at[1], rt.at[2 - c], p0s.at[2], p0r.at[2 - c], chip_dev(adj_chip, 1))
    send(wt.at[0], rt.at[0], p0s.at[0], p0r.at[0], partner)
    loads[3].wait()
    loads[13].wait()
    spot_row = lax.broadcasted_iota(jnp.int32, (4, 256), 0)
    spot_lane = lax.broadcasted_iota(jnp.int32, (4, 256), 1)

    def mask_leaf(t, carry):
        v = win[32 + t]
        win[32 + t] = jnp.where((spot_row == 3) & (spot_lane >= live_ref[t]), 0.0, v)
        return carry

    lax.fori_loop(0, 32, mask_leaf, 0, unroll=4)

    up_d, down_d = (d + 1) % 256, (d + 255) % 256
    up_dev, down_dev = (up_d // 32, up_d % 32), (down_d // 32, down_d % 32)
    own = win.at[pl.ds(32, 32)]
    send(own, win.at[pl.ds(0, 32)], hs.at[0], hr.at[0], up_dev)
    send(own, win.at[pl.ds(64, 32)], hs.at[1], hr.at[1], down_dev)
    send(dens_hbm, dw.at[pl.ds(0, 32)], hs.at[2], hr.at[2], up_dev)
    send(dens_hbm, dw.at[pl.ds(64, 32)], hs.at[3], hr.at[3], down_dev)

    def target_step(t, carry):
        v = jnp.where(spot_row < 3, win[32 + t], 0.0)
        for i, piece in enumerate(target_rows(v)):
            fa[4 * i : 4 * i + 4, 0:256] = piece
        tfeat[t] = jnp.transpose(fa[:, 0:256]).astype(jnp.bfloat16)
        tfar[t] = fa[:, 0:256].astype(jnp.bfloat16)
        return carry

    fa[40:PARTS, :] = jnp.zeros((PARTS - 40, 1024), jnp.float32)
    fb[40:PARTS, :] = jnp.zeros((PARTS - 40, 1024), jnp.float32)
    lax.fori_loop(0, 32, target_step, 0, unroll=4)
    loads[9].wait()
    far_points = surf

    def pull_step(t, carry):
        pulls[t] = lax.rsqrt(dot_n(far_points[...], tfar[t]))
        return carry

    lax.fori_loop(0, 32, pull_step, 0, unroll=8)

    for k in range(3):
        arrive(rt.at[k], p0r.at[k])
    total = wt[0] + rt[0] + rt[1] + rt[2]
    tile = jnp.where(c == 0, total[:, 0:128], total[:, 128:256])
    tail = jnp.where(c == 0, total[0:4, 256:384], total[4:8, 256:384])
    pv_ref[c, b, a, z, 0] = tile[0:4]
    pv_ref[c, b, a, z, 1] = tile[4:8]
    pv_ref[c, b, a, z, 2] = tail
    for k in (4, 3, 5, 2, 6, 1, 7):
        spot = pv_ref.at[c, b, a, z]
        send(spot, spot, zs.at[k - 1], zr.at[k - 1], ((z + k) % 8, gy))

    def prepare(t, feat, charge):
        for n in range(4):
            leaf = near_ref[n, t]
            v = win[jnp.clip(leaf - 32 * d + 32, 0, 95)]
            gap = jnp.where(spot_row == 0, leaf % 32 - t, 0)
            gap = jnp.where(spot_row == 1, (leaf // 32) % 32 - d % 32, gap)
            gap = jnp.where(spot_row == 2, leaf // 1024 - d // 32, gap)
            placed = jnp.where(spot_row < 3, v + 2.0 * gap.astype(jnp.float32), SOFT**0.5)
            for i, piece in enumerate(source_rows(placed)):
                feat[4 * i : 4 * i + 4, 256 * n : 256 * n + 256] = piece
            charge[0:1, 256 * n : 256 * n + 256] = v[3:4]

    def weigh(points, others, weights):
        count = others.shape[1]
        sums = []
        for i in range(0, 256, 64):
            pulled = lax.rsqrt(dot_n(points[i : i + 64], others)) * weights
            acc = pulled[:, 0:128]
            for j in range(128, count, 128):
                acc = acc + pulled[:, j : j + 128]
            sums.append(acc)
        return jnp.sum(jnp.transpose(jnp.concatenate(sums, axis=0)), axis=0, keepdims=True)

    def near_leaf(t, feat, charge):
        near_rows[pl.ds(t, 1), :] = weigh(tfeat[t], feat[...].astype(jnp.bfloat16), charge[0:1, :])

    def near_pair(i, carry):
        t = 2 * i
        prepare(t + 1, fb, qb)
        near_leaf(t, fa, qa)
        prepare(jnp.minimum(t + 2, 31), fa, qa)
        near_leaf(t + 1, fb, qb)
        return carry

    def near_part(k):
        if NEAR_SPLIT[k] < NEAR_SPLIT[k + 1]:
            lax.fori_loop(NEAR_SPLIT[k] // 2, NEAR_SPLIT[k + 1] // 2, near_pair, 0, unroll=2)

    for load in loads[4:9] + loads[10:13]:
        load.wait()

    def split_step(i, carry):
        v = trans[i]
        at = pl.ds(pl.multiple_of(256 * i, 256), 256)
        th[:, at], tl[:, at] = halves(v[:, 0:256])
        return carry

    lax.fori_loop(0, 16, split_step, 0, unroll=2)
    lane = lax.broadcasted_iota(jnp.int32, (P_SIZE, 128), 1)
    blank = jnp.zeros((P_SIZE, 88), jnp.float32)
    for i in range(0, 16, 3):
        packed = jnp.zeros((P_SIZE, 128), jnp.float32)
        for m in range(min(3, 16 - i)):
            piece = jnp.concatenate([trans[i + m, :, 256:P_SIZE], blank], axis=1)
            packed = packed + (pltpu.roll(piece, 40 * m, 1) if m else piece)
        at = 4096 + 128 * (i // 3)
        th[:, at : at + 128], tl[:, at : at + 128] = halves(packed)
    for k in range(2):
        arrive(win.at[pl.ds(64 * k, 32)], hr.at[k])
    prepare(0, fa, qa)
    near_part(0)

    for k in (1, 7, 2, 6, 3, 5, 4):
        arrive(pv_ref.at[c, b, a, (z + 8 - k) % 8], zr.at[k - 1])
    forwards = 0

    def forward(spot):
        nonlocal forwards
        send(spot, spot, fs.at[forwards], fr.at[forwards], partner)
        forwards += 1

    spot = pv_ref.at[c, b, a]
    for k in (2, 1, 3):
        send(spot, spot, as_.at[k - 1], ar.at[k - 1], ab_dev((a + k) % 4, b))
    for k in (1, 3):
        send(spot, spot, bs.at[0, k - 1], br.at[0, k - 1], ab_dev(a, (b + k) % 4))
    forward(spot)

    near_part(1)

    for j in (1, 3, 2):
        spot = pv_ref.at[c, b, (a + 4 - j) % 4]
        arrive(spot, ar.at[j - 1])
        for k in (1, 3):
            send(spot, spot, bs.at[j, k - 1], br.at[j, k - 1], ab_dev(a, (b + k) % 4))
        forward(spot)

    def b_step(j):
        for k in (1, 3):
            spot = pv_ref.at[c, (b + 4 - k) % 4, (a + 4 - j) % 4]
            arrive(spot, br.at[j, k - 1])
            if (j in (0, 3)) == (k == 1):
                send(spot, spot, bs.at[j, 1], br.at[j, 1], ab_dev(a, (b + k) % 4))
            forward(spot)

    near_part(2)
    b_step(0)
    near_part(3)
    b_step(1)
    near_part(4)
    b_step(3)
    near_part(5)
    b_step(2)
    for k in range(2):
        arrive(dw.at[pl.ds(64 * k, 32)], hr.at[2 + k])

    def columns(ref):
        return jnp.transpose(ref[...])

    def choose(cols, count, width):
        lane = lax.broadcasted_iota(jnp.int32, (32, width), 1)
        return jnp.concatenate(
            [(cols[:, k : k + 1] == lane).astype(jnp.float32) for k in range(count)], axis=0
        ).astype(jnp.bfloat16)

    def by_class(ref, count):
        table = ref[...]
        pad = jnp.zeros((count, 96), jnp.int32)
        wide = jnp.concatenate([table, pad], axis=1)
        tiles = []
        for k in range(0, count, 4):
            row = wide[k : k + 1]
            for m in range(1, 4):
                row = row + pltpu.roll(wide[k + m : k + m + 1], 32 * m, 1)
            tiles.append(row)
        row = jnp.concatenate(tiles, axis=1)
        shape = (512, 32 * count)
        line = lax.broadcasted_iota(jnp.int32, shape, 0)
        lane = lax.broadcasted_iota(jnp.int32, shape, 1)
        code = row * 32 + lax.broadcasted_iota(jnp.int32, row.shape, 1) % 32
        return jnp.where(code == line, 1.0, 0.0).astype(jnp.bfloat16)

    far_pick = choose(columns(flist) - 32 * d + 32, 16, 96)
    dens_high, dens_low = halves(dw[...])
    far_high = dot_n(far_pick, dens_high).astype(jnp.bfloat16)
    far_low = dot_n(far_pick, dens_low).astype(jnp.bfloat16)
    far_class = by_class(fclass, 16)
    gfar[...] = jnp.zeros_like(gfar)
    gfar[:, 0:P_SIZE] = dot_n(far_class, far_high) + dot_n(far_class, far_low)

    wanted = clist[...]
    spots = ((wanted // 8) % 16) * 64 + (wanted // 128) * 8 + wanted % 8
    coarse_pick = choose(jnp.transpose(spots), 8, 1024)
    coarse_class = by_class(cclass, 8)
    down_high, down_low = halves(down[...])

    for j in (0, 1, 3, 2):
        spot = pv_ref.at[c, (b + 2) % 4, (a + 4 - j) % 4]
        arrive(spot, br.at[j, 1])
        forward(spot)

    arrive(pv_ref.at[1 - c, a, b], fr.at[0])
    n = 1
    for j in (1, 3, 2):
        arrive(pv_ref.at[1 - c, a, (b + 4 - j) % 4], fr.at[n])
        n += 1
    for j in (0, 1, 3, 2):
        for k in (1, 3):
            arrive(pv_ref.at[1 - c, (a + 4 - k) % 4, (b + 4 - j) % 4], fr.at[n])
            n += 1

    def collect(da, db):
        a1, b1 = (a + da) % 4, (b + db) % 4
        xx, yy = a1 + c * (b1 - a1), b1 + c * (a1 - b1)
        base = (xx * 4 + yy) * 64
        for k in range(4):
            parts = []
            for zz in (2 * k, 2 * k + 1):
                one, two_ = pv_ref[0, yy, xx, zz], pv_ref[1, xx, yy, zz]
                parts.append(
                    jnp.concatenate(
                        [
                            jnp.concatenate([one[0], one[1]], axis=0),
                            jnp.concatenate([two_[0], two_[1]], axis=0),
                            jnp.concatenate([one[2], two_[2]], axis=0),
                        ],
                        axis=1,
                    )
                )
            high, low = halves(jnp.concatenate(parts, axis=0))
            at = pl.ds(pl.multiple_of(base + 16 * k, 16), 16)
            up_high[at, :] = high
            up_low[at, :] = low

    def collect_near(i, carry):
        p, q = i // 3, i % 3
        collect(p + p // 2, q + q // 2)
        return carry

    def collect_far(i, carry):
        collect(2, i)
        return carry

    def collect_side(i, carry):
        collect(i + i // 2, 2)
        return carry

    lax.fori_loop(0, 9, collect_near, 0, unroll=3)
    for j in (0, 1, 3, 2):
        arrive(pv_ref.at[1 - c, (a + 2) % 4, (b + 4 - j) % 4], fr.at[n])
        n += 1
    lax.fori_loop(0, 4, collect_far, 0, unroll=2)
    lax.fori_loop(0, 3, collect_side, 0, unroll=3)
    coarse_high = dot_n(coarse_pick, up_high[...]).astype(jnp.bfloat16)
    coarse_low = dot_n(coarse_pick, up_low[...]).astype(jnp.bfloat16)
    gathered = gfar[...] + dot_n(coarse_class, coarse_high) + dot_n(coarse_class, coarse_low)
    ends = []
    for i in range(0, 16, 3):
        packed = gathered[32 * i : 32 * i + 32, 256:384]
        for m in range(1, min(3, 16 - i)):
            packed = packed + pltpu.roll(gathered[32 * (i + m) : 32 * (i + m) + 32, 256:384], 40 * m, 1)
        ends.append(packed)
    spread = jnp.concatenate([gathered[32 * i : 32 * i + 32, 0:256] for i in range(16)] + ends, axis=1)
    g_high, g_low = halves(spread)
    wide_sum = dot_t(th[...], jnp.concatenate([g_high, g_low], axis=0))
    check = wide_sum[:, 0:32] + wide_sum[:, 32:64] + dot_t(tl[...], g_high)
    c_high, c_low = halves(check)
    equiv = dot_n(down_high, c_high) + dot_n(down_high, c_low) + dot_n(down_low, c_high)
    for t in range(32):
        far = jnp.sum(equiv[:, t : t + 1] * pulls[t], axis=0, keepdims=True)
        out_ref[t : t + 1, :] = near_rows[t : t + 1, :] + far
    for cp in sends:
        cp.wait_send()


def surface_features():
    points = np.concatenate([surface_rows(), np.full((1, P_SIZE), SOFT**0.5, np.float32)], axis=0)

    def short(v):
        return v.astype(jnp.bfloat16).astype(np.float32)

    high = short(points)
    low = short(points - high)
    seen = high + low
    square = seen * seen
    s1 = short(square)
    s2 = short(square - s1)
    s3 = short(square - s1 - s2)
    one = np.ones_like(points)
    rows = [-2 * high, -2 * low, -2 * high, -2 * low, s1, s2, s3, one, one, one]
    stacked = np.concatenate(rows + [np.zeros((PARTS - 40, P_SIZE), np.float32)], axis=0)
    return np.ascontiguousarray(stacked.T).astype(jnp.bfloat16)


def on_device(
    sources, live_counts, densities, near_list, far_list, far_class, coarse_list, coarse_class, translations,
    check_to_equiv, up_check_to_equiv, partial_check, contrib_ids,
):
    hbm = pl.BlockSpec(memory_space=pl.ANY)
    vmem = pl.BlockSpec(memory_space=pltpu.VMEM)
    dma = pltpu.SemaphoreType.DMA
    f32, bf16, i32 = jnp.float32, jnp.bfloat16, jnp.int32
    sums = pl.pallas_call(
        fmm_kernel,
        out_shape=jax.ShapeDtypeStruct((32, 256), f32),
        in_specs=[hbm] * 14,
        out_specs=vmem,
        scratch_shapes=[
            pltpu.VMEM((2, 4, 4, 8, 3, 4, 128), f32),
            pltpu.VMEM((2, 8, 384), f32),
            pltpu.VMEM((3, 8, 384), f32),
            pltpu.VMEM((96, 4, 256), f32),
            pltpu.VMEM((96, P_SIZE), f32),
            pltpu.VMEM((16, 32), i32),
            pltpu.VMEM((16, 32), i32),
            pltpu.VMEM((8, 32), i32),
            pltpu.VMEM((8, 32), i32),
            pltpu.VMEM((16, P_SIZE, P_SIZE), f32),
            pltpu.VMEM((P_SIZE, P_SIZE), f32),
            pltpu.VMEM((P_SIZE, P_SIZE), f32),
            pltpu.VMEM((64, P_SIZE), f32),
            pltpu.VMEM((1, 64), i32),
            pltpu.VMEM((P_SIZE, PARTS), bf16),
            pltpu.VMEM((32, 256, PARTS), bf16),
            pltpu.VMEM((32, PARTS, 256), bf16),
            pltpu.VMEM((PARTS, 1024), f32),
            pltpu.VMEM((PARTS, 1024), f32),
            pltpu.VMEM((8, 1024), f32),
            pltpu.VMEM((8, 1024), f32),
            pltpu.VMEM((P_SIZE, 4864), bf16),
            pltpu.VMEM((P_SIZE, 4864), bf16),
            pltpu.VMEM((512, 384), f32),
            pltpu.VMEM((1024, 384), bf16),
            pltpu.VMEM((1024, 384), bf16),
            pltpu.VMEM((32, P_SIZE, 256), f32),
            pltpu.VMEM((32, 256), f32),
            pltpu.SMEM((4, 32), i32),
            pltpu.SMEM((32,), i32),
            dma((3,)), dma((3,)), dma((4,)), dma((4,)), dma((7,)), dma((7,)),
            dma((3,)), dma((3,)), dma((4, 3)), dma((4, 3)), dma((16,)), dma((16,)), dma((14,)),
        ],
        compiler_params=pltpu.CompilerParams(
            collective_id=0, has_side_effects=True, vmem_limit_bytes=57 * 1024 * 1024
        ),
    )(
        near_list.T, live_counts, sources, densities.T, far_list.T, far_class.T, coarse_list.T, coarse_class.T,
        translations, check_to_equiv, up_check_to_equiv, partial_check[0].T, contrib_ids,
        jnp.asarray(surface_features()),
    )
    return jnp.where(jnp.arange(256, dtype=jnp.int32)[None, :] < live_counts[:, None], sums, 0.0)


def solution(mesh):
    both = ("gx", "gy")
    return jax.shard_map(
        on_device,
        mesh=mesh,
        in_specs=(
            P(both, None, None), P(both), P(None, both), P(both, None), P(both, None), P(both, None), P(both, None),
            P(both, None), P(), P(), P(), P(both, None, None), P(both, None),
        ),
        out_specs=P(both, None),
        check_vma=False,
    )
```
